1024 devices in a mesh: gx: 32 (over x_hi, z), gy: 32 (over x_lo, y, core).
Axes of the slice: x: 4 (x_hi: 2, x_lo: 2; x = x_hi * 2 + x_lo), y: 8, z: 16, core: 2. Of those that a mesh axis runs over, the one named last changes fastest.
Arguments:
- velocity: float32 [3, 8, 1024, 4096], P(None, None, 'gx', 'gy'), may hold values from -6 to 6
- stress: float32 [6, 8, 1024, 4096], P(None, None, 'gx', 'gy'), may hold values from -6 to 6
- zones: int32 [8, 1024, 4096], P(None, 'gx', 'gy'), may hold values from 0 to 15
- zone_table: float32 [3, 16], replicated, may hold values from 0.5 to 2
- regional: float32 [32, 2, 3, 32, 8192], P('gx', None, None, None, 'gy'), may hold values from -6 to 6
- owner: int32 [32], replicated, may hold values from 0 to 31
- footprint_building: int32 [32, 32, 64], P('gx', 'gy'), may hold values from 0 to 1023
- footprint_block: int32 [32, 32, 64], P('gx', 'gy'), may hold values from 0 to 63
Outputs:
- velocity_out: float32 [3, 8, 1024, 4096], P(None, None, 'gx', 'gy')
- stress_out: float32 [6, 8, 1024, 4096], P(None, None, 'gx', 'gy')
- base_shear: float32 [2, 1024], replicated
The draws below stay inside these ranges and needn't reach their ends.
All inputs are finite; a program needn't handle non-finite values.
Results may differ from the reference program's by a relative error of at most 0.000084.
Values sent between devices are 32-bit elements; how exact they have to be, the bound alone decides.
A program may use at most 32 MiB of HBM per device.

```python
import jax
import jax.numpy as jnp

CX = 32
CY = 128
NZ = 8
STEPS = 2
COARSE = 4
BLOCK = 8
ZONES = 16
BUILDINGS = 1024
FP_DEV = 64
NX = 1024
NY = 4096
CXC = 8
CYC = 32
BLOCKS_DEV = 64
N_GX = 32
N_GY = 32


def draw_owner(key, part):
    first = jax.random.fold_in(key, 11)
    second = jax.random.fold_in(key, 23)
    values = jax.random.randint(first, (N_GY,), 0, N_GX)
    where = jax.random.randint(second, (), 0, N_GY)
    return values.at[where].set(N_GX - 1).astype(jnp.int32)


def set_ends(entries, stream_key, least, high):
    longest = entries.shape.index(max(entries.shape))
    spots = []
    for shift in (0, 1):
        where = [jax.random.randint(jax.random.fold_in(stream_key, axis), (), 0, length) for axis, length in enumerate(entries.shape)]
        where[longest] = (where[longest] + shift) % entries.shape[longest]
        spots.append(tuple(where))
    return entries.at[spots[0]].set(least).at[spots[1]].set(high)


def block_levels(key, extent, split, least, high):
    loudness = 1.0
    for dim, parts in split:
        steps = jax.random.uniform(jax.random.fold_in(jax.random.fold_in(key, 6), dim), (parts,), jnp.float32, least / len(split), high / len(split))
        loudness = loudness * jnp.repeat(jnp.exp(steps), extent[dim] // parts).reshape((-1,) + (1,) * (len(extent) - 1 - dim))
    return loudness


def bell_draw(rng, dims, width, limit, cuts=(), held_as=jnp.bfloat16):
    gain = block_levels(rng, dims, cuts, -0.22, 0.18) if cuts else 1.0
    array = jax.random.normal(rng, dims, jnp.float32) * width * gain
    return jnp.minimum(jnp.maximum(array, -limit), limit).astype(held_as)


def setup_inputs(seed: int = 0) -> dict:
    splits = jax.random.split(jax.random.key(seed), 9)
    return {
        "velocity": bell_draw(splits[0], (3, NZ, NX, NY), 1.0, 6.0, ((2, 32), (3, 32)), jnp.float32),
        "stress": bell_draw(splits[1], (6, NZ, NX, NY), 1.0, 6.0, ((2, 32), (3, 32)), jnp.float32),
        "zones": set_ends(jax.random.randint(splits[2], (NZ, NX, NY), 0, ZONES), jax.random.fold_in(splits[2], 1), 0, ZONES - 1).astype(jnp.int32),
        "zone_table": jnp.clip(jax.random.uniform(splits[3], (3, ZONES), jnp.float32, 0.5, 2.0), 0.5, 2.0),
        "regional": bell_draw(splits[4], (N_GX, STEPS, 3, N_GX, N_GY * CXC * CYC), 1.0, 6.0, ((0, 32), (4, 32)), jnp.float32),
        "owner": draw_owner(jax.random.fold_in(splits[8], 71), 0),
        "footprint_building": set_ends(jax.random.randint(splits[6], (N_GX, N_GY, FP_DEV), 0, BUILDINGS), jax.random.fold_in(splits[6], 1), 0, BUILDINGS - 1).astype(jnp.int32),
        "footprint_block": set_ends(jax.random.randint(splits[7], (N_GX, N_GY, FP_DEV), 0, BLOCKS_DEV), jax.random.fold_in(splits[7], 1), 0, BLOCKS_DEV - 1).astype(jnp.int32),
    }


def diff_x(field):
    return (jnp.roll(field, -1, axis=1) - jnp.roll(field, 1, axis=1)) * 0.5


def diff_y(field):
    return (jnp.roll(field, -1, axis=2) - jnp.roll(field, 1, axis=2)) * 0.5


def diff_z(field):
    padded = jnp.pad(field, ((1, 1), (0, 0), (0, 0)))
    return (padded[2:] - padded[:-2]) * 0.5


def reference(velocity, stress, zones, zone_table, regional, owner, footprint_building, footprint_block):
    lam = zone_table[0][zones]
    shear_mod = zone_table[1][zones]
    buoy = zone_table[2][zones]
    shaped = regional.reshape(N_GX, STEPS, 3, N_GX, N_GY, CXC, CYC)
    shaped = jnp.moveaxis(shaped, 4, 0)
    picked = shaped[jnp.arange(N_GY), owner.astype(jnp.int32)]
    picked = jnp.transpose(picked, (1, 2, 3, 4, 0, 5)).reshape(STEPS, 3, N_GX * CXC, N_GY * CYC)
    drm = jnp.repeat(jnp.repeat(picked, COARSE, axis=2), COARSE, axis=3)
    for step in range(STEPS):
        sxx, sxz, sxy, syy, syz, szz = stress[0], stress[1], stress[2], stress[3], stress[4], stress[5]
        force_x = diff_x(sxx) + diff_y(sxy) + diff_z(sxz)
        force_y = diff_x(sxy) + diff_y(syy) + diff_z(syz)
        force_z = diff_x(sxz) + diff_y(syz) + diff_z(szz)
        force = jnp.stack([force_x, force_y, force_z])
        force = force.at[:, NZ - 1].add(shear_mod[NZ - 1][None] * drm[step])
        velocity = velocity + 0.2 * buoy[None] * force
        vx, vy, vz = velocity[0], velocity[1], velocity[2]
        dvx_dx = diff_x(vx)
        dvy_dy = diff_y(vy)
        dvz_dz = diff_z(vz)
        theta = dvx_dx + dvy_dy + dvz_dz
        new_xx = sxx + 0.2 * (lam * theta + 2.0 * shear_mod * dvx_dx)
        new_xz = sxz + 0.2 * shear_mod * (diff_z(vx) + diff_x(vz))
        new_xy = sxy + 0.2 * shear_mod * (diff_y(vx) + diff_x(vy))
        new_yy = syy + 0.2 * (lam * theta + 2.0 * shear_mod * dvy_dy)
        new_yz = syz + 0.2 * shear_mod * (diff_z(vy) + diff_y(vz))
        new_zz = szz + 0.2 * (lam * theta + 2.0 * shear_mod * dvz_dz)
        stress = jnp.stack([new_xx, new_xz, new_xy, new_yy, new_yz, new_zz])
    plane = jnp.stack([stress[1, 1], stress[4, 1]])
    plane = plane.reshape(2, N_GX, CX // BLOCK, BLOCK, N_GY, CY // BLOCK, BLOCK)
    means = jnp.sum(plane, axis=(3, 6)) * (1.0 / (BLOCK * BLOCK))
    means = jnp.transpose(means, (0, 1, 3, 2, 4)).reshape(2, N_GX, N_GY, BLOCKS_DEV)
    rows = jnp.arange(N_GX)[:, None, None]
    cols = jnp.arange(N_GY)[None, :, None]
    values = means[:, rows, cols, footprint_block.astype(jnp.int32)]
    shear = jnp.zeros((2, BUILDINGS), jnp.float32)
    shear = shear.at[:, footprint_building.reshape(-1)].add(values.reshape(2, -1))
    return velocity, stress, shear
```

```python
import functools

import jax
import jax.numpy as jnp
from jax import lax
from jax.experimental import pallas as pl
from jax.experimental.pallas import tpu as pltpu
from jax.sharding import PartitionSpec as P

CX = 32
CY = 128
NZ = 8
STEPS = 2
COARSE = 4
BLOCK = 8
ZONES = 16
BUILDINGS = 1024
LANES = 128
PAD = 8
ROWS = 2 * BUILDINGS // LANES
MESH = pl.DeviceIdType.MESH
HIGH = lax.Precision.HIGHEST
F32 = jnp.float32

XX, XZ, XY, YY, YZ, ZZ = range(6)


def lane_of(shape):
    return lax.broadcasted_iota(jnp.int32, shape, len(shape) - 1)


def row_of(shape):
    return lax.broadcasted_iota(jnp.int32, shape, len(shape) - 2)


def kernel(
    owner, table, vel, stress_in, zones, regional, buildings, blocks,
    vel_out, stress_out, shear,
    S, V, lam, mu, buoy, drm, counts,
    xs, xr, ys, yr, reg_send, reg_recv, part, r1, q1, r2, q2, gathered,
    load_sem, store_sem, halo_send, halo_recv, reg_sems, sum_sems,
):
    GX, GY = lax.axis_size("gx"), lax.axis_size("gy")
    gx, gy = lax.axis_index("gx"), lax.axis_index("gy")
    nz_own = part.shape[0]

    core = pl.ds(PAD, CX)
    load_v = pltpu.make_async_copy(vel, V.at[:, :, core, :], load_sem.at[0])
    load_s = pltpu.make_async_copy(stress_in, S.at[:, :, core, :], load_sem.at[1])
    load_s.start()
    load_v.start()

    barrier = pltpu.get_barrier_semaphore()

    def greet_x(d, carry):
        pl.semaphore_signal(barrier, inc=1, device_id=((gx + d) % GX, gy), device_id_type=MESH)
        return carry

    def greet_y(d, carry):
        pl.semaphore_signal(barrier, inc=1, device_id=(gx, (gy + d) % GY), device_id_type=MESH)
        return carry

    lax.fori_loop(1, GX, greet_x, 0)
    lax.fori_loop(1, GY, greet_y, 0)

    def pack_regional(i, carry):
        for s in range(STEPS):
            for c in range(3):
                reg_send[i, s * 3 + c, 0:1, :] = regional[0, s, c, pl.ds(i, 1), :]
        return carry

    lax.fori_loop(0, GX, pack_regional, 0)

    lane = lane_of((CX, CY))
    first_lane = lane == 0
    last_lane = lane == CY - 1
    pair = lane >> 1
    odd = (lane & 1) == 1

    def exchange(r, ref, fx, fy, z0, z1):
        n = z1 - z0
        for k, f in enumerate(fx):
            xs[r, 0, k, 0:n, :] = ref[f, z0:z1, PAD, :]
            xs[r, 1, k, 0:n, :] = ref[f, z0:z1, PAD + CX - 1, :]
        acc = jnp.zeros((CX, CY), F32)
        m = 0
        for f in fy:
            for z in range(z0, z1):
                moved = pltpu.roll(ref[f, z, core, :], 2 * m + 1, 1)
                acc = jnp.where(pair == m, moved, acc)
                m += 1
        ys[r] = acc
        copies = []
        for d, (src, dst, to) in enumerate([
            (xs.at[r, 0], xr.at[r, 0], ((gx + GX - 1) % GX, gy)),
            (xs.at[r, 1], xr.at[r, 1], ((gx + 1) % GX, gy)),
            (ys.at[r], yr.at[r, 0], (gx, (gy + GY - 1) % GY)),
            (ys.at[r], yr.at[r, 1], (gx, (gy + 1) % GY)),
        ]):
            copy = pltpu.make_async_remote_copy(
                src_ref=src, dst_ref=dst, send_sem=halo_send.at[r, d],
                recv_sem=halo_recv.at[r, d], device_id=to, device_id_type=MESH)
            copies.append(copy)
        return copies

    def start(copies):
        for copy in copies:
            copy.start()

    def arrive(copies, r, ref, fx, z0, z1):
        n = z1 - z0
        for copy in copies:
            copy.wait_recv()
        for k, f in enumerate(fx):
            ref[f, z0:z1, PAD + CX, :] = xr[r, 0, k, 0:n, :]
            ref[f, z0:z1, PAD - 1, :] = xr[r, 1, k, 0:n, :]
        from_right = pltpu.roll(yr[r, 0], CY - 1, 1)
        from_left = pltpu.roll(yr[r, 1], 1, 1)
        return jnp.where(odd, from_left, from_right)

    def diff_x(ref, f, z):
        return ref[f, z, pl.ds(PAD + 1, CX), :] - ref[f, z, pl.ds(PAD - 1, CX), :]

    def diff_y(ref, f, z, edge, m):
        value = ref[f, z, core, :]
        moved = pltpu.roll(edge, CY - (2 * m + 1), 1)
        after = jnp.where(last_lane, moved, pltpu.roll(value, CY - 1, 1))
        before = jnp.where(first_lane, moved, pltpu.roll(value, 1, 1))
        return after - before

    def diff_z(ref, f, z):
        if z == 0:
            return ref[f, 1, core, :]
        if z == NZ - 1:
            return -ref[f, NZ - 2, core, :]
        return ref[f, z + 1, core, :] - ref[f, z - 1, core, :]

    def velocity_planes(step, edge, e0, e1, z0, z1):
        ne = e1 - e0
        for z in range(z0, z1):
            k = z - e0
            b = buoy[z]
            force = [
                diff_x(S, XX, z) + diff_y(S, XY, z, edge, k) + diff_z(S, XZ, z),
                diff_x(S, XY, z) + diff_y(S, YY, z, edge, ne + k) + diff_z(S, YZ, z),
                diff_x(S, XZ, z) + diff_y(S, YZ, z, edge, 2 * ne + k) + diff_z(S, ZZ, z),
            ]
            for c in range(3):
                f = force[c]
                if z == NZ - 1:
                    f = f + 20.0 * mu[z] * drm[step * 3 + c]
                V[c, z, core, :] = V[c, z, core, :] + b * f

    def stress_planes(edge, e0, e1, z0, z1):
        ne = e1 - e0
        for z in range(z0, z1):
            k = z - e0
            m1 = mu[z]
            dvx = diff_x(V, 0, z)
            dvy = diff_y(V, 1, z, edge, ne + k)
            dvz = diff_z(V, 2, z)
            common = lam[z] * (dvx + dvy + dvz)
            m2 = m1 + m1
            S[XX, z, core, :] = S[XX, z, core, :] + (common + m2 * dvx)
            S[YY, z, core, :] = S[YY, z, core, :] + (common + m2 * dvy)
            S[ZZ, z, core, :] = S[ZZ, z, core, :] + (common + m2 * dvz)
            S[XZ, z, core, :] = S[XZ, z, core, :] + m1 * (diff_z(V, 0, z) + diff_x(V, 2, z))
            S[XY, z, core, :] = S[XY, z, core, :] + m1 * (diff_y(V, 0, z, edge, k) + diff_x(V, 1, z))
            S[YZ, z, core, :] = S[YZ, z, core, :] + m1 * (diff_z(V, 1, z) + diff_y(V, 2, z, edge, 2 * ne + k))

    SX, SY, VX, VY = (XX, XY, XZ), (XY, YY, YZ), (0, 1, 2), (0, 1, 2)

    load_s.wait()
    c0 = exchange(0, S, SX, SY, 0, NZ)
    pl.semaphore_wait(barrier, GX + GY - 2)
    start(c0)

    reg_slot = gx

    def send_regional(d, carry):
        to = (gx + d) % GX
        pltpu.make_async_remote_copy(
            src_ref=reg_send.at[to], dst_ref=reg_recv.at[reg_slot], send_sem=reg_sems.at[0],
            recv_sem=reg_sems.at[1], device_id=(to, gy), device_id_type=MESH).start()
        return carry

    lax.fori_loop(1, GX, send_regional, 0)
    reg_recv[reg_slot] = reg_send[gx]

    for z in range(NZ):
        zone = zones[z]
        bits = [(zone & (1 << b)) != 0 for b in range(4)]
        for row, target in ((0, lam), (1, mu), (2, buoy)):
            level = [table[row, t] * 0.1 for t in range(ZONES)]
            for b in range(4):
                level = [
                    jnp.where(bits[b], level[2 * t + 1], level[2 * t]) for t in range(len(level) // 2)
                ]
            target[z] = level[0]

    n_blocks = (CX // BLOCK) * (CY // BLOCK)
    entries = blocks.shape[-1]
    block_hot = (blocks[0] == row_of((n_blocks, entries))).astype(jnp.bfloat16)
    building_hot = (buildings[0] == row_of((BUILDINGS, entries))).astype(jnp.bfloat16)
    counts[...] = lax.dot_general(
        block_hot, building_hot, (((1,), (1,)), ((), ())), preferred_element_type=F32)

    load_v.wait()

    def whole(src, dst, send_sem, recv_sem):
        return pltpu.make_async_remote_copy(
            src_ref=src, dst_ref=dst, send_sem=send_sem, recv_sem=recv_sem,
            device_id=((gx + 1) % GX, gy), device_id_type=MESH)

    all_regional = whole(
        reg_send.at[pl.ds(0, GX - 1)], reg_recv.at[pl.ds(0, GX - 1)], reg_sems.at[0], reg_sems.at[1])

    def take_regional():
        all_regional.wait_recv()
        root = owner[gy]
        wide = (CX, 2 * LANES)
        mine = reg_recv[root]
        keep = (lane_of(wide) >> 5) == (row_of(wide) >> 2)
        rows = jnp.concatenate(
            [jnp.where(keep, jnp.broadcast_to(mine[q], wide), 0.0) for q in range(6)], axis=0)
        spread_shape = (2 * LANES, CY)
        spread = ((row_of(spread_shape) & 31) == (lane_of(spread_shape) >> 2)).astype(F32)
        plane = jnp.dot(rows, spread, precision=HIGH, preferred_element_type=F32)
        for q in range(6):
            drm[q] = plane[q * CX:(q + 1) * CX, :]

    started = []

    def round_trip(r, ref, fx, fy, z0, z1):
        copies = exchange(r, ref, fx, fy, z0, z1)
        start(copies)
        started.append(copies)
        return copies

    started.append(c0)

    e0 = arrive(c0, 0, S, SX, 0, NZ)
    velocity_planes(0, e0, 0, NZ, 0, 5)
    c = round_trip(1, V, VX, VY, 0, 5)
    e1 = arrive(c, 1, V, VX, 0, 5)
    velocity_rest = (5, NZ)
    take_regional()
    velocity_planes(0, e0, 0, NZ, *velocity_rest)
    c_b1 = round_trip(2, V, VX, VY, 5, NZ)
    stress_planes(e1, 0, 5, 0, 4)
    c = round_trip(3, S, SX, SY, 0, 4)
    e2 = arrive(c, 3, S, SX, 0, 4)
    eb1 = arrive(c_b1, 2, V, VX, 5, NZ)
    stress_planes(e1, 0, 5, 4, 5)
    stress_planes(eb1, 5, NZ, 5, NZ)
    c_b2 = round_trip(4, S, SX, SY, 4, NZ)
    velocity_planes(1, e2, 0, 4, 0, 3)
    c = round_trip(5, V, VX, VY, 0, 3)
    e3 = arrive(c, 5, V, VX, 0, 3)
    eb2 = arrive(c_b2, 4, S, SX, 4, NZ)
    velocity_planes(1, e2, 0, 4, 3, 4)
    velocity_planes(1, eb2, 4, NZ, 4, NZ)
    c_b3 = round_trip(6, V, VX, VY, 3, NZ)
    save_v = pltpu.make_async_copy(V.at[:, :, core, :], vel_out, store_sem.at[0])
    save_v.start()
    stress_planes(e3, 0, 3, 0, 3)

    sums = jnp.concatenate(
        [jnp.sum(S[f, 1, core, :].reshape(CX // BLOCK, BLOCK, CY), axis=1) for f in (XZ, YZ)], axis=0)
    fold_shape = (CY, n_blocks)
    fold = ((row_of(fold_shape) >> 3) == (lane_of(fold_shape) & 15)).astype(F32)
    per_block = jnp.dot(sums, fold, precision=HIGH, preferred_element_type=F32)
    mask_shape = (8, n_blocks)
    own_row = (row_of(mask_shape) & 3) == (lane_of(mask_shape) >> 4)
    per_block = jnp.where(own_row, per_block, 0.0) * (1.0 / (BLOCK * BLOCK))
    total = jnp.dot(per_block, counts[...], precision=HIGH, preferred_element_type=F32)
    per_owner = ROWS // nz_own
    for comp in range(2):
        row = jnp.sum(total[4 * comp:4 * comp + 4], axis=0, keepdims=True)
        for t in range(BUILDINGS // LANES):
            k = comp * (BUILDINGS // LANES) + t
            part[k // per_owner, k % per_owner] = row[:, t * LANES:(t + 1) * LANES]

    mine_row = gx % nz_own

    def send_part(d, carry):
        to = (gx + d) % GX
        pltpu.make_async_remote_copy(
            src_ref=part.at[to % nz_own], dst_ref=r1.at[gx], send_sem=sum_sems.at[0],
            recv_sem=sum_sems.at[1], device_id=(to, gy), device_id_type=MESH).start()
        return carry

    lax.fori_loop(1, GX, send_part, 0)
    r1[gx] = part[mine_row]
    wait_r1 = whole(r1.at[pl.ds(0, GX - 1)], r1.at[pl.ds(0, GX - 1)], sum_sems.at[0], sum_sems.at[1])
    wait_r1.wait_recv()
    q1[...] = jnp.sum(r1[...], axis=0)

    def send_row(d, carry):
        to = (gy + d) % GY
        pltpu.make_async_remote_copy(
            src_ref=q1, dst_ref=r2.at[gy], send_sem=sum_sems.at[2],
            recv_sem=sum_sems.at[3], device_id=(gx, to), device_id_type=MESH).start()
        return carry

    lax.fori_loop(1, GY, send_row, 0)
    r2[gy] = q1[...]
    wait_r2 = whole(r2.at[pl.ds(0, GY - 1)], r2.at[pl.ds(0, GY - 1)], sum_sems.at[2], sum_sems.at[3])

    eb3 = arrive(c_b3, 6, V, VX, 3, NZ)
    stress_planes(eb3, 3, NZ, 3, NZ)
    save_s = pltpu.make_async_copy(S.at[:, :, core, :], stress_out, store_sem.at[1])
    save_s.start()

    wait_r2.wait_recv()
    q2[...] = jnp.sum(r2[...], axis=0)

    base = gx - mine_row

    def send_total(d, carry):
        to = base + (mine_row + d) % nz_own
        pltpu.make_async_remote_copy(
            src_ref=q2, dst_ref=gathered.at[mine_row], send_sem=sum_sems.at[4],
            recv_sem=sum_sems.at[5], device_id=(to, gy), device_id_type=MESH).start()
        return carry

    lax.fori_loop(1, nz_own, send_total, 0)
    gathered[mine_row] = q2[...]
    some = pl.ds(0, nz_own - 1)
    wait_g = whole(gathered.at[some], gathered.at[some], sum_sems.at[4], sum_sems.at[5])
    wait_g.wait_recv()
    for comp in range(2):
        for t in range(BUILDINGS // LANES):
            k = comp * (BUILDINGS // LANES) + t
            shear[comp:comp + 1, t * LANES:(t + 1) * LANES] = gathered[k // per_owner, k % per_owner]

    for copies in started:
        for copy in copies:
            copy.wait_send()
    all_regional.wait_send()
    wait_r1.wait_send()
    wait_r2.wait_send()
    wait_g.wait_send()
    save_v.wait()
    save_s.wait()


def body(velocity, stress, zones, zone_table, regional, owner, footprint_building, footprint_block):
    GX, GY = lax.axis_size("gx"), lax.axis_size("gy")
    nz_own = min(GX, ROWS)
    per_owner = ROWS // nz_own
    rounds = 7
    vmem = pl.BlockSpec(memory_space=pltpu.VMEM)
    smem = pl.BlockSpec(memory_space=pltpu.SMEM)
    hbm = pl.BlockSpec(memory_space=pl.ANY)
    dma = pltpu.SemaphoreType.DMA
    return pl.pallas_call(
        kernel,
        out_shape=(
            jax.ShapeDtypeStruct(velocity.shape, F32),
            jax.ShapeDtypeStruct(stress.shape, F32),
            jax.ShapeDtypeStruct((2, BUILDINGS), F32),
        ),
        in_specs=[smem, smem, hbm, hbm, vmem, vmem, vmem, vmem],
        out_specs=(hbm, hbm, vmem),
        scratch_shapes=[
            pltpu.VMEM((6, NZ, CX + 2 * PAD, CY), F32),
            pltpu.VMEM((3, NZ, CX + 2 * PAD, CY), F32),
            pltpu.VMEM((NZ, CX, CY), F32),
            pltpu.VMEM((NZ, CX, CY), F32),
            pltpu.VMEM((NZ, CX, CY), F32),
            pltpu.VMEM((6, CX, CY), F32),
            pltpu.VMEM((64, BUILDINGS), F32),
            pltpu.VMEM((rounds, 2, 3, NZ, CY), F32),
            pltpu.VMEM((rounds, 2, 3, NZ, CY), F32),
            pltpu.VMEM((rounds, CX, CY), F32),
            pltpu.VMEM((rounds, 2, CX, CY), F32),
            pltpu.VMEM((GX, 6, 1, 2 * LANES), F32),
            pltpu.VMEM((GX, 6, 1, 2 * LANES), F32),
            pltpu.VMEM((nz_own, per_owner, 1, LANES), F32),
            pltpu.VMEM((GX, per_owner, 1, LANES), F32),
            pltpu.VMEM((per_owner, 1, LANES), F32),
            pltpu.VMEM((GY, per_owner, 1, LANES), F32),
            pltpu.VMEM((per_owner, 1, LANES), F32),
            pltpu.VMEM((nz_own, per_owner, 1, LANES), F32),
            dma((2,)),
            dma((2,)),
            dma((rounds, 4)),
            dma((rounds, 4)),
            dma((2,)),
            dma((6,)),
        ],
        compiler_params=pltpu.CompilerParams(
            collective_id=0, has_side_effects=True, vmem_limit_bytes=32 * 1024 * 1024
        ),
    )(owner, zone_table, velocity, stress, zones, regional, footprint_building, footprint_block)


def solution(mesh):
    return jax.shard_map(
        body,
        mesh=mesh,
        in_specs=(
            P(None, None, "gx", "gy"),
            P(None, None, "gx", "gy"),
            P(None, "gx", "gy"),
            P(),
            P("gx", None, None, None, "gy"),
            P(),
            P("gx", "gy", None),
            P("gx", "gy", None),
        ),
        out_specs=(P(None, None, "gx", "gy"), P(None, None, "gx", "gy"), P()),
        check_vma=False,
    )
```

```python
import functools

import jax
import jax.numpy as jnp
from jax import lax
from jax.experimental import pallas as pl
from jax.experimental.pallas import tpu as pltpu
from jax.sharding import PartitionSpec as P

CX = 32
CY = 128
NZ = 8
STEPS = 2
COARSE = 4
BLOCK = 8
ZONES = 16
BUILDINGS = 1024
LANES = 128
PAD = 8
ROWS = 2 * BUILDINGS // LANES
MESH = pl.DeviceIdType.MESH
HIGH = lax.Precision.HIGHEST
F32 = jnp.float32

XX, XZ, XY, YY, YZ, ZZ = range(6)


def lane_of(shape):
    return lax.broadcasted_iota(jnp.int32, shape, len(shape) - 1)


def row_of(shape):
    return lax.broadcasted_iota(jnp.int32, shape, len(shape) - 2)


def layers(gx_size):
    z_size = min(gx_size, 16)
    return z_size, gx_size // z_size


def kernel(
    owner_hbm, table_hbm, vel, stress_in, zones_hbm, regional_hbm, buildings_hbm, blocks_hbm,
    vel_out, stress_out, shear,
    S, V, lam, mu, buoy, drm, counts,
    xs, xr, ys, yr, reg_send, reg_recv, part, r1, q1, hub, q2, gathered,
    owner, table, zones, regional, buildings, blocks,
    load_sem, store_sem, halo_send, halo_recv, reg_sems, sum_sems, entered, beside,
):
    GX, GY = lax.axis_size("gx"), lax.axis_size("gy")
    gx, gy = lax.axis_index("gx"), lax.axis_index("gy")
    z_size, x_size = layers(GX)
    owners = part.shape[0]
    z_me = gx % z_size
    base_x = gx - z_me

    def rank_of(g):
        return (g % z_size) * x_size + g // z_size

    def at_rank(q):
        return (q % x_size) * z_size + q // x_size

    me = rank_of(gx)

    core = pl.ds(PAD, CX)
    loads = [
        pltpu.make_async_copy(src, dst, load_sem.at[k]) for k, (src, dst) in enumerate([
            (stress_in, S.at[:, :, core, :]), (vel, V.at[:, :, core, :]), (regional_hbm, regional),
            (zones_hbm, zones), (table_hbm, table), (owner_hbm, owner), (buildings_hbm, buildings),
            (blocks_hbm, blocks),
        ])
    ]
    for load in loads:
        load.start()

    barrier = pltpu.get_barrier_semaphore()

    def greet_x(q, carry):
        pl.semaphore_signal(barrier, inc=1, device_id=(at_rank(q), gy), device_id_type=MESH)
        return carry

    def greet_y(d, carry):
        pl.semaphore_signal(barrier, inc=1, device_id=(gx, (gy + d) % GY), device_id_type=MESH)
        return carry

    lax.fori_loop(1, GY, greet_y, 0)
    lax.fori_loop(me + 1, GX, greet_x, 0)

    lane = lane_of((CX, CY))
    first_lane = lane == 0
    last_lane = lane == CY - 1
    pair = lane >> 1
    odd = (lane & 1) == 1

    def exchange(r, ref, fx, fy, z0, z1):
        n = z1 - z0
        for k, f in enumerate(fx):
            xs[r, 0, k, 0:n, :] = ref[f, z0:z1, PAD, :]
            xs[r, 1, k, 0:n, :] = ref[f, z0:z1, PAD + CX - 1, :]
        acc = jnp.zeros((CX, CY), F32)
        m = 0
        for f in fy:
            for z in range(z0, z1):
                moved = pltpu.roll(ref[f, z, core, :], 2 * m + 1, 1)
                acc = jnp.where(pair == m, moved, acc)
                m += 1
        ys[r] = acc
        copies = []
        for d, (src, dst, to) in enumerate([
            (xs.at[r, 0], xr.at[r, 0], ((gx + GX - 1) % GX, gy)),
            (xs.at[r, 1], xr.at[r, 1], ((gx + 1) % GX, gy)),
            (ys.at[r], yr.at[r, 0], (gx, (gy + GY - 1) % GY)),
            (ys.at[r], yr.at[r, 1], (gx, (gy + 1) % GY)),
        ]):
            copy = pltpu.make_async_remote_copy(
                src_ref=src, dst_ref=dst, send_sem=halo_send.at[r, d],
                recv_sem=halo_recv.at[r, d], device_id=to, device_id_type=MESH)
            copies.append(copy)
        return copies

    def start(copies):
        for copy in copies:
            copy.start()

    def arrive(copies, r, ref, fx, z0, z1):
        n = z1 - z0
        for copy in copies:
            copy.wait_recv()
        for k, f in enumerate(fx):
            ref[f, z0:z1, PAD + CX, :] = xr[r, 0, k, 0:n, :]
            ref[f, z0:z1, PAD - 1, :] = xr[r, 1, k, 0:n, :]
        from_right = pltpu.roll(yr[r, 0], CY - 1, 1)
        from_left = pltpu.roll(yr[r, 1], 1, 1)
        return jnp.where(odd, from_left, from_right)

    def diff_x(ref, f, z):
        return ref[f, z, pl.ds(PAD + 1, CX), :] - ref[f, z, pl.ds(PAD - 1, CX), :]

    def diff_y(ref, f, z, edge, m):
        value = ref[f, z, core, :]
        moved = pltpu.roll(edge, CY - (2 * m + 1), 1)
        after = jnp.where(last_lane, moved, pltpu.roll(value, CY - 1, 1))
        before = jnp.where(first_lane, moved, pltpu.roll(value, 1, 1))
        return after - before

    def diff_z(ref, f, z):
        if z == 0:
            return ref[f, 1, core, :]
        if z == NZ - 1:
            return -ref[f, NZ - 2, core, :]
        return ref[f, z + 1, core, :] - ref[f, z - 1, core, :]

    def velocity_planes(step, edge, e0, e1, z0, z1):
        ne = e1 - e0
        for z in range(z0, z1):
            k = z - e0
            b = buoy[z]
            force = [
                diff_x(S, XX, z) + diff_y(S, XY, z, edge, k) + diff_z(S, XZ, z),
                diff_x(S, XY, z) + diff_y(S, YY, z, edge, ne + k) + diff_z(S, YZ, z),
                diff_x(S, XZ, z) + diff_y(S, YZ, z, edge, 2 * ne + k) + diff_z(S, ZZ, z),
            ]
            for c in range(3):
                f = force[c]
                if z == NZ - 1:
                    f = f + 20.0 * mu[z] * drm[step * 3 + c]
                V[c, z, core, :] = V[c, z, core, :] + b * f

    def stress_planes(edge, e0, e1, z0, z1):
        ne = e1 - e0
        for z in range(z0, z1):
            k = z - e0
            m1 = mu[z]
            dvx = diff_x(V, 0, z)
            dvy = diff_y(V, 1, z, edge, ne + k)
            dvz = diff_z(V, 2, z)
            common = lam[z] * (dvx + dvy + dvz)
            m2 = m1 + m1
            S[XX, z, core, :] = S[XX, z, core, :] + (common + m2 * dvx)
            S[YY, z, core, :] = S[YY, z, core, :] + (common + m2 * dvy)
            S[ZZ, z, core, :] = S[ZZ, z, core, :] + (common + m2 * dvz)
            S[XZ, z, core, :] = S[XZ, z, core, :] + m1 * (diff_z(V, 0, z) + diff_x(V, 2, z))
            S[XY, z, core, :] = S[XY, z, core, :] + m1 * (diff_y(V, 0, z, edge, k) + diff_x(V, 1, z))
            S[YZ, z, core, :] = S[YZ, z, core, :] + m1 * (diff_z(V, 1, z) + diff_y(V, 2, z, edge, 2 * ne + k))

    SX, SY, VX, VY = (XX, XY, XZ), (XY, YY, YZ), (0, 1, 2), (0, 1, 2)

    loads[0].wait()
    c0 = exchange(0, S, SX, SY, 0, NZ)
    pl.semaphore_wait(barrier, me + GY - 1)

    after, before = (gx + 1) % GX, (gx + GX - 1) % GX

    @pl.when(rank_of(after) < me)
    def _():
        pl.semaphore_signal(beside.at[1], inc=1, device_id=(after, gy), device_id_type=MESH)

    @pl.when(rank_of(before) < me)
    def _():
        pl.semaphore_signal(beside.at[0], inc=1, device_id=(before, gy), device_id_type=MESH)

    @pl.when(rank_of(before) < me)
    def _():
        c0[0].start()

    @pl.when(rank_of(after) < me)
    def _():
        c0[1].start()

    c0[2].start()
    c0[3].start()

    def answer(q, carry):
        pl.semaphore_signal(entered.at[me], inc=1, device_id=(at_rank(q), gy), device_id_type=MESH)
        return carry

    lax.fori_loop(0, me, answer, 0)

    loads[2].wait()

    def pack_regional(i, carry):
        for s in range(STEPS):
            for c in range(3):
                reg_send[i, s * 3 + c, 0:1, :] = regional[0, s, c, pl.ds(i, 1), :]
        return carry

    lax.fori_loop(0, GX, pack_regional, 0)

    def send_regional(q):
        to = at_rank(q)
        pltpu.make_async_remote_copy(
            src_ref=reg_send.at[to], dst_ref=reg_recv.at[gx], send_sem=reg_sems.at[0],
            recv_sem=reg_sems.at[1], device_id=(to, gy), device_id_type=MESH).start()

    def send_lower(q, carry):
        send_regional(q)
        return carry

    def send_higher(q, carry):
        pl.semaphore_wait(entered.at[q], 1)
        send_regional(q)
        return carry

    lax.fori_loop(0, me, send_lower, 0)
    reg_recv[gx] = reg_send[gx]
    near = jnp.minimum(me + 1 + 3 * x_size, GX)
    middle = jnp.minimum(me + 1 + 5 * x_size, GX)

    @pl.when(rank_of(before) > me)
    def _():
        pl.semaphore_wait(beside.at[1], 1)
        c0[0].start()

    @pl.when(rank_of(after) > me)
    def _():
        pl.semaphore_wait(beside.at[0], 1)
        c0[1].start()

    for k in (3, 4, 6, 7):
        loads[k].wait()

    for z in range(NZ):
        zone = zones[z]
        bits = [(zone & (1 << b)) != 0 for b in range(4)]
        for row, target in ((0, lam), (1, mu), (2, buoy)):
            level = [table[row, t] * 0.1 for t in range(ZONES)]
            for b in range(4):
                level = [
                    jnp.where(bits[b], level[2 * t + 1], level[2 * t]) for t in range(len(level) // 2)
                ]
            target[z] = level[0]

    n_blocks = (CX // BLOCK) * (CY // BLOCK)
    entries = blocks.shape[-1]
    block_hot = (blocks[0] == row_of((n_blocks, entries))).astype(jnp.bfloat16)
    building_hot = (buildings[0] == row_of((BUILDINGS, entries))).astype(jnp.bfloat16)
    counts[...] = lax.dot_general(
        block_hot, building_hot, (((1,), (1,)), ((), ())), preferred_element_type=F32)

    loads[1].wait()
    loads[5].wait()
    lax.fori_loop(me + 1, near, send_higher, 0)

    def whole(src, dst, send_sem, recv_sem):
        return pltpu.make_async_remote_copy(
            src_ref=src, dst_ref=dst, send_sem=send_sem, recv_sem=recv_sem,
            device_id=((gx + 1) % GX, gy), device_id_type=MESH)

    all_regional = whole(
        reg_send.at[pl.ds(0, GX - 1)], reg_recv.at[pl.ds(0, GX - 1)], reg_sems.at[0], reg_sems.at[1])

    def take_regional():
        all_regional.wait_recv()
        root = owner[gy]
        wide = (CX, 2 * LANES)
        mine = reg_recv[root]
        keep = (lane_of(wide) >> 5) == (row_of(wide) >> 2)
        rows = jnp.concatenate(
            [jnp.where(keep, jnp.broadcast_to(mine[q], wide), 0.0) for q in range(6)], axis=0)
        spread_shape = (2 * LANES, CY)
        spread = ((row_of(spread_shape) & 31) == (lane_of(spread_shape) >> 2)).astype(F32)
        plane = jnp.dot(rows, spread, precision=HIGH, preferred_element_type=F32)
        for q in range(6):
            drm[q] = plane[q * CX:(q + 1) * CX, :]

    started = []

    def round_trip(r, ref, fx, fy, z0, z1):
        copies = exchange(r, ref, fx, fy, z0, z1)
        start(copies)
        started.append(copies)
        return copies

    started.append(c0)

    e0 = arrive(c0, 0, S, SX, 0, NZ)
    velocity_planes(0, e0, 0, NZ, 0, 5)
    c = round_trip(1, V, VX, VY, 0, 5)
    lax.fori_loop(near, middle, send_higher, 0)
    e1 = arrive(c, 1, V, VX, 0, 5)
    stress_planes(e1, 0, 5, 0, 4)
    c = round_trip(3, S, SX, SY, 0, 4)
    e2 = arrive(c, 3, S, SX, 0, 4)
    velocity_planes(1, e2, 0, 4, 0, 3)
    c = round_trip(5, V, VX, VY, 0, 3)
    e3 = arrive(c, 5, V, VX, 0, 3)
    stress_planes(e3, 0, 3, 0, 2)

    sums = jnp.concatenate(
        [jnp.sum(S[f, 1, core, :].reshape(CX // BLOCK, BLOCK, CY), axis=1) for f in (XZ, YZ)], axis=0)
    fold_shape = (CY, n_blocks)
    fold = ((row_of(fold_shape) >> 3) == (lane_of(fold_shape) & 15)).astype(F32)
    per_block = jnp.dot(sums, fold, precision=HIGH, preferred_element_type=F32)
    mask_shape = (8, n_blocks)
    own_row = (row_of(mask_shape) & 3) == (lane_of(mask_shape) >> 4)
    per_block = jnp.where(own_row, per_block, 0.0) * (1.0 / (BLOCK * BLOCK))
    total = jnp.dot(per_block, counts[...], precision=HIGH, preferred_element_type=F32)
    per_owner = ROWS // owners
    for comp in range(2):
        row = jnp.sum(total[4 * comp:4 * comp + 4], axis=0, keepdims=True)
        for t in range(BUILDINGS // LANES):
            k = comp * (BUILDINGS // LANES) + t
            part[k // per_owner, k % per_owner] = row[:, t * LANES:(t + 1) * LANES]

    my_row = gy % owners

    def send_part(d, carry):
        to = (gy + d) % GY
        pltpu.make_async_remote_copy(
            src_ref=part.at[to % owners], dst_ref=r1.at[gy], send_sem=sum_sems.at[0],
            recv_sem=sum_sems.at[1], device_id=(gx, to), device_id_type=MESH).start()
        return carry

    lax.fori_loop(1, GY, send_part, 0)
    r1[gy] = part[my_row]
    lax.fori_loop(middle, GX, send_higher, 0)
    peers_y = pl.ds(0, GY - 1)
    wait_r1 = whole(r1.at[peers_y], r1.at[peers_y], sum_sems.at[0], sum_sems.at[1])
    wait_r1.wait_recv()
    q1[...] = jnp.sum(r1[...], axis=0)

    is_hub = z_me == 0
    for x in range(x_size):
        @pl.when(gx != x * z_size)
        def _():
            pltpu.make_async_remote_copy(
                src_ref=q1, dst_ref=hub.at[gx], send_sem=sum_sems.at[2],
                recv_sem=sum_sems.at[3], device_id=(x * z_size, gy), device_id_type=MESH).start()

    take_regional()
    velocity_planes(0, e0, 0, NZ, 5, NZ)
    c = round_trip(2, V, VX, VY, 5, NZ)
    eb1 = arrive(c, 2, V, VX, 5, NZ)
    stress_planes(e1, 0, 5, 4, 5)
    stress_planes(eb1, 5, NZ, 5, NZ)
    c = round_trip(4, S, SX, SY, 4, NZ)

    peers_x = pl.ds(0, GX - 1)
    wait_hub = whole(hub.at[peers_x], hub.at[peers_x], sum_sems.at[2], sum_sems.at[3])

    def send_down(z, carry):
        pltpu.make_async_remote_copy(
            src_ref=q2, dst_ref=q2, send_sem=sum_sems.at[4],
            recv_sem=sum_sems.at[5], device_id=(base_x + z, gy), device_id_type=MESH).start()
        return carry

    down = whole(q2, q2, sum_sems.at[4], sum_sems.at[5])

    @pl.when(is_hub)
    def _():
        hub[gx] = q1[...]
        wait_hub.wait_recv()
        q2[...] = jnp.sum(hub[...], axis=0)
        lax.fori_loop(1, z_size, send_down, 0)

    @pl.when(z_me != 0)
    def _():
        down.wait_recv()

    base = gy - my_row

    def send_total(d, carry):
        to = base + (my_row + d) % owners
        pltpu.make_async_remote_copy(
            src_ref=q2, dst_ref=gathered.at[my_row], send_sem=sum_sems.at[6],
            recv_sem=sum_sems.at[7], device_id=(gx, to), device_id_type=MESH).start()
        return carry

    lax.fori_loop(1, owners, send_total, 0)
    gathered[my_row] = q2[...]

    eb2 = arrive(c, 4, S, SX, 4, NZ)
    velocity_planes(1, e2, 0, 4, 3, 4)
    velocity_planes(1, eb2, 4, NZ, 4, NZ)
    c = round_trip(6, V, VX, VY, 3, NZ)
    save_v = pltpu.make_async_copy(V.at[:, :, core, :], vel_out, store_sem.at[0])
    save_v.start()
    stress_planes(e3, 0, 3, 2, 3)

    some = pl.ds(0, owners - 1)
    wait_g = whole(gathered.at[some], gathered.at[some], sum_sems.at[6], sum_sems.at[7])
    wait_g.wait_recv()
    for comp in range(2):
        for t in range(BUILDINGS // LANES):
            k = comp * (BUILDINGS // LANES) + t
            shear[comp:comp + 1, t * LANES:(t + 1) * LANES] = gathered[k // per_owner, k % per_owner]

    eb3 = arrive(c, 6, V, VX, 3, NZ)
    stress_planes(eb3, 3, NZ, 3, NZ)
    save_s = pltpu.make_async_copy(S.at[:, :, core, :], stress_out, store_sem.at[1])
    save_s.start()

    for copies in started:
        for copy in copies:
            copy.wait_send()
    all_regional.wait_send()
    wait_r1.wait_send()
    for x in range(x_size):
        @pl.when(gx != x * z_size)
        def _():
            down_like = whole(q1, q1, sum_sems.at[2], sum_sems.at[3])
            down_like.wait_send()

    @pl.when(is_hub)
    def _():
        low = whole(
            hub.at[pl.ds(0, z_size - 1)], hub.at[pl.ds(0, z_size - 1)], sum_sems.at[4], sum_sems.at[5])
        low.wait_send()

    wait_g.wait_send()
    save_v.wait()
    save_s.wait()


def body(velocity, stress, zones, zone_table, regional, owner, footprint_building, footprint_block):
    GX, GY = lax.axis_size("gx"), lax.axis_size("gy")
    owners = min(GY, ROWS)
    per_owner = ROWS // owners
    rounds = 7
    vmem = pl.BlockSpec(memory_space=pltpu.VMEM)
    hbm = pl.BlockSpec(memory_space=pltpu.HBM)
    dma = pltpu.SemaphoreType.DMA
    return pl.pallas_call(
        kernel,
        out_shape=(
            jax.ShapeDtypeStruct(velocity.shape, F32),
            jax.ShapeDtypeStruct(stress.shape, F32),
            jax.ShapeDtypeStruct((2, BUILDINGS), F32),
        ),
        in_specs=[hbm] * 8,
        out_specs=(hbm, hbm, vmem),
        scratch_shapes=[
            pltpu.VMEM((6, NZ, CX + 2 * PAD, CY), F32),
            pltpu.VMEM((3, NZ, CX + 2 * PAD, CY), F32),
            pltpu.VMEM((NZ, CX, CY), F32),
            pltpu.VMEM((NZ, CX, CY), F32),
            pltpu.VMEM((NZ, CX, CY), F32),
            pltpu.VMEM((6, CX, CY), F32),
            pltpu.VMEM((64, BUILDINGS), F32),
            pltpu.VMEM((rounds, 2, 3, NZ, CY), F32),
            pltpu.VMEM((rounds, 2, 3, NZ, CY), F32),
            pltpu.VMEM((rounds, CX, CY), F32),
            pltpu.VMEM((rounds, 2, CX, CY), F32),
            pltpu.VMEM((GX, 6, 1, 2 * LANES), F32),
            pltpu.VMEM((GX, 6, 1, 2 * LANES), F32),
            pltpu.VMEM((owners, per_owner, 1, LANES), F32),
            pltpu.VMEM((GY, per_owner, 1, LANES), F32),
            pltpu.VMEM((per_owner, 1, LANES), F32),
            pltpu.VMEM((GX, per_owner, 1, LANES), F32),
            pltpu.VMEM((per_owner, 1, LANES), F32),
            pltpu.VMEM((owners, per_owner, 1, LANES), F32),
            pltpu.SMEM(owner.shape, owner.dtype),
            pltpu.SMEM(zone_table.shape, zone_table.dtype),
            pltpu.VMEM(zones.shape, zones.dtype),
            pltpu.VMEM(regional.shape, regional.dtype),
            pltpu.VMEM(footprint_building.shape, footprint_building.dtype),
            pltpu.VMEM(footprint_block.shape, footprint_block.dtype),
            dma((8,)),
            dma((2,)),
            dma((rounds, 4)),
            dma((rounds, 4)),
            dma((2,)),
            dma((8,)),
            pltpu.SemaphoreType.REGULAR((GX,)),
            pltpu.SemaphoreType.REGULAR((2,)),
        ],
        compiler_params=pltpu.CompilerParams(
            collective_id=0, has_side_effects=True, vmem_limit_bytes=60 * 1024 * 1024
        ),
    )(owner, zone_table, velocity, stress, zones, regional, footprint_building, footprint_block)


def solution(mesh):
    return jax.shard_map(
        body,
        mesh=mesh,
        in_specs=(
            P(None, None, "gx", "gy"),
            P(None, None, "gx", "gy"),
            P(None, "gx", "gy"),
            P(),
            P("gx", None, None, None, "gy"),
            P(),
            P("gx", "gy", None),
            P("gx", "gy", None),
        ),
        out_specs=(P(None, None, "gx", "gy"), P(None, None, "gx", "gy"), P()),
        check_vma=False,
    )
```

```python
import functools

import jax
import jax.numpy as jnp
from jax import lax
from jax.experimental import pallas as pl
from jax.experimental.pallas import tpu as pltpu
from jax.sharding import PartitionSpec as P

CX = 32
CY = 128
NZ = 8
STEPS = 2
COARSE = 4
BLOCK = 8
ZONES = 16
BUILDINGS = 1024
LANES = 128
PAD = 8
WIDE = 4
HIGH_ROWS = CX + 2 * PAD
GROUP = 16
ROWS = 2 * BUILDINGS // LANES
MESH = pl.DeviceIdType.MESH
HIGH = lax.Precision.HIGHEST
F32 = jnp.float32

XX, XZ, XY, YY, YZ, ZZ = range(6)


def lane_of(shape):
    return lax.broadcasted_iota(jnp.int32, shape, len(shape) - 1)


def row_of(shape):
    return lax.broadcasted_iota(jnp.int32, shape, len(shape) - 2)


def layers(gx_size):
    z_size = min(gx_size, 16)
    return z_size, gx_size // z_size


def kernel(
    owner_hbm, table_hbm, vel, stress_in, zones_hbm, regional_hbm, buildings_hbm, blocks_hbm,
    vel_out, stress_out, shear,
    S, V, lam, mu, buoy, drm, counts,
    xs, xr, ys, yr, corner, packed, block, reg_send, reg_recv, part, r1, q1, hub, q2, gathered,
    owner, table, zones, regional, buildings, blocks,
    load_sem, store_sem, halo_send, halo_recv, block_send, block_recv, reg_sems, sum_sems, entered, beside,
):
    GX, GY = lax.axis_size("gx"), lax.axis_size("gy")
    gx, gy = lax.axis_index("gx"), lax.axis_index("gy")
    z_size, x_size = layers(GX)
    owners = part.shape[0]
    z_me = gx % z_size
    base_x = gx - z_me

    def rank_of(g):
        return (g % z_size) * x_size + g // z_size

    def at_rank(q):
        return (q % x_size) * z_size + q // x_size

    me = rank_of(gx)

    core = pl.ds(PAD, CX)
    loads = [
        pltpu.make_async_copy(src, dst, load_sem.at[k]) for k, (src, dst) in enumerate([
            (stress_in, S.at[:, :, 0, core, :]), (vel, V.at[:, :, 0, core, :]), (regional_hbm, regional),
            (zones_hbm, zones), (table_hbm, table), (owner_hbm, owner), (buildings_hbm, buildings),
            (blocks_hbm, blocks),
        ])
    ]
    for load in loads:
        load.start()

    barrier = pltpu.get_barrier_semaphore()

    def greet_x(q, carry):
        pl.semaphore_signal(barrier, inc=1, device_id=(at_rank(q), gy), device_id_type=MESH)
        return carry

    def greet_y(d, carry):
        pl.semaphore_signal(barrier, inc=1, device_id=(gx, (gy + d) % GY), device_id_type=MESH)
        return carry

    after, before = (gx + 1) % GX, (gx + GX - 1) % GX
    right, left = (gy + 1) % GY, (gy + GY - 1) % GY
    sides = ((before, rank_of(before)), (after, rank_of(after)))

    for next_x, rank in sides:
        @pl.when(rank > me)
        def _():
            for y in (left, right):
                pl.semaphore_signal(barrier, inc=1, device_id=(next_x, y), device_id_type=MESH)

    lax.fori_loop(1, GY, greet_y, 0)
    lax.fori_loop(me + 1, GX, greet_x, 0)

    lane = lane_of((CX, CY))
    wide_lane = lane_of((CX + 2 * WIDE, CY))

    fields = {"s": S, "v": V, "zone": zones}
    s_planes = [("s", f, z) for f in range(6) for z in range(NZ)]
    v_planes = [("v", f, z) for f in range(3) for z in range(NZ)]
    z_planes = [("zone", 0, z) for z in range(NZ)]
    y_planes = s_planes + v_planes + z_planes

    def needed_early(plane):
        name, f, z = plane
        return z < 5 or (name == "s" and f in (XZ, YZ, ZZ) and z < 6)

    early = [p for p in y_planes if needed_early(p)]
    late = [p for p in y_planes if not needed_early(p)]
    x_planes = early + late
    n_early = len(early)

    def rows_of(plane, r, n):
        name, f, z = plane
        if name == "zone":
            return zones[z, r:r + n, :].astype(F32)
        return fields[name][f, z, 0, PAD + r:PAD + r + n, :]

    for k in (0, 1, 3):
        loads[k].wait()
    for k, plane in enumerate(x_planes):
        xs[0, k] = rows_of(plane, 0, WIDE)
        xs[1, k] = rows_of(plane, CX - WIDE, WIDE)
    for g in range(len(y_planes) // GROUP):
        acc = jnp.zeros((CX, CY), F32)
        for k in range(GROUP):
            moved = pltpu.roll(rows_of(y_planes[g * GROUP + k], 0, CX), 2 * WIDE * k + WIDE, 1)
            acc = jnp.where((lane >> 3) == k, moved, acc)
        ys[g] = acc

    e_part, l_part = pl.ds(0, n_early), pl.ds(n_early, len(late))
    top, bottom = pl.ds(0, 8), pl.ds(CX - 8, 8)
    halo = [
        pltpu.make_async_remote_copy(
            src_ref=src, dst_ref=dst, send_sem=halo_send.at[k], recv_sem=halo_recv.at[k],
            device_id=to, device_id_type=MESH)
        for k, (src, dst, to) in enumerate([
            (xs.at[0, e_part], xr.at[0, e_part], (before, gy)),
            (xs.at[1, e_part], xr.at[1, e_part], (after, gy)),
            (xs.at[0, l_part], xr.at[0, l_part], (before, gy)),
            (xs.at[1, l_part], xr.at[1, l_part], (after, gy)),
            (ys, yr.at[0], (gx, left)),
            (ys, yr.at[1], (gx, right)),
            (ys.at[:, top, :], corner.at[0, 1], (before, left)),
            (ys.at[:, top, :], corner.at[0, 0], (before, right)),
            (ys.at[:, bottom, :], corner.at[1, 1], (after, left)),
            (ys.at[:, bottom, :], corner.at[1, 0], (after, right)),
        ])
    ]
    by_side = ((0, 6, 7, 2), (1, 8, 9, 3))

    lower = [(rank < me).astype(jnp.int32) for _, rank in sides]
    pl.semaphore_wait(barrier, me + GY - 1 + 2 * (lower[0] + lower[1]))

    for side, (next_x, rank) in enumerate(sides):
        @pl.when(rank < me)
        def _():
            for k, y in enumerate((right, gy, left)):
                pl.semaphore_signal(
                    beside.at[1 - side, k], inc=1, device_id=(next_x, y), device_id_type=MESH)

    for side, (next_x, rank) in enumerate(sides):
        @pl.when(rank < me)
        def _():
            for k in by_side[side]:
                halo[k].start()

    halo[4].start()
    halo[5].start()

    def answer(q, carry):
        pl.semaphore_signal(entered.at[me], inc=1, device_id=(at_rank(q), gy), device_id_type=MESH)
        return carry

    lax.fori_loop(0, me, answer, 0)

    loads[2].wait()

    def pack_regional(i, carry):
        for s in range(STEPS):
            for c in range(3):
                reg_send[i, s * 3 + c, 0:1, :] = regional[0, s, c, pl.ds(i, 1), :]
        return carry

    lax.fori_loop(0, GX, pack_regional, 0)

    def send_regional(q):
        to = at_rank(q)
        pltpu.make_async_remote_copy(
            src_ref=reg_send.at[to], dst_ref=reg_recv.at[gx], send_sem=reg_sems.at[0],
            recv_sem=reg_sems.at[1], device_id=(to, gy), device_id_type=MESH).start()

    def send_lower(q, carry):
        send_regional(q)
        return carry

    def send_higher(q, carry):
        pl.semaphore_wait(entered.at[q], 1)
        send_regional(q)
        return carry

    lax.fori_loop(0, me, send_lower, 0)
    reg_recv[gx] = reg_send[gx]
    near = jnp.minimum(me + 1 + 3 * x_size, GX)

    for side, (next_x, rank) in enumerate(sides):
        @pl.when(rank > me)
        def _():
            for k in range(3):
                pl.semaphore_wait(beside.at[side, k], 1)
            for k in by_side[side]:
                halo[k].start()

    for k in (4, 5, 6, 7):
        loads[k].wait()

    def lookup(zone):
        bits = [(zone & (1 << b)) != 0 for b in range(4)]
        found = []
        for row in range(3):
            level = [table[row, t] * 0.1 for t in range(ZONES)]
            for b in range(4):
                level = [
                    jnp.where(bits[b], level[2 * t + 1], level[2 * t]) for t in range(len(level) // 2)
                ]
            found.append(level[0])
        return found

    materials = (lam, mu, buoy)
    for z in range(NZ):
        for target, value in zip(materials, lookup(zones[z])):
            target[z, 0, core, :] = value

    n_blocks = (CX // BLOCK) * (CY // BLOCK)
    entries = blocks.shape[-1]
    block_hot = (blocks[0] == row_of((n_blocks, entries))).astype(jnp.bfloat16)
    building_hot = (buildings[0] == row_of((BUILDINGS, entries))).astype(jnp.bfloat16)
    counts[...] = lax.dot_general(
        block_hot, building_hot, (((1,), (1,)), ((), ())), preferred_element_type=F32)

    lax.fori_loop(me + 1, near, send_higher, 0)

    def whole(src, dst, send_sem, recv_sem):
        return pltpu.make_async_remote_copy(
            src_ref=src, dst_ref=dst, send_sem=send_sem, recv_sem=recv_sem,
            device_id=((gx + 1) % GX, gy), device_id_type=MESH)

    all_regional = whole(
        reg_send.at[pl.ds(0, GX - 1)], reg_recv.at[pl.ds(0, GX - 1)], reg_sems.at[0], reg_sems.at[1])

    around = [(dx, dy) for dx in (-1, 0, 1) for dy in (-1, 0, 1) if (dx, dy) != (0, 0)]
    x_at, y_at = {-1: before, 0: gx, 1: after}, {-1: left, 0: gy, 1: right}
    share = [
        pltpu.make_async_remote_copy(
            src_ref=block.at[1, 1], dst_ref=block.at[1 - dx, 1 - dy], send_sem=block_send.at[k],
            recv_sem=block_recv.at[k], device_id=(x_at[dx], y_at[dy]), device_id_type=MESH)
        for k, (dx, dy) in enumerate(around)
    ]

    def share_block():
        all_regional.wait_recv()
        block[1, 1] = reg_recv[owner[gy]]
        for copy in share:
            copy.start()

    def spread_blocks():
        for copy in share:
            copy.wait_recv()
        wide = (HIGH_ROWS, 2 * LANES)
        row = row_of(wide)
        keep = (lane_of(wide) >> 5) == (((row - PAD) >> 2) & 7)

        def stack(y):
            parts = []
            for q in range(6):
                above, own, below = [jnp.broadcast_to(block[x, y, q], wide) for x in range(3)]
                value = jnp.where(row < PAD, above, jnp.where(row < PAD + CX, own, below))
                parts.append(jnp.where(keep, value, 0.0))
            return jnp.concatenate(parts, axis=0)

        shape = (2 * LANES, CY)
        cell, out = row_of(shape) & 31, lane_of(shape)
        own = (cell == (out >> 2)).astype(F32)
        from_left = ((cell == 31) & (out >= CY - WIDE)).astype(F32)
        from_right = ((cell == 0) & (out < WIDE)).astype(F32)
        dot = functools.partial(jnp.dot, precision=HIGH, preferred_element_type=F32)
        middle = dot(stack(1), own)
        edges = dot(stack(0), from_left) + dot(stack(2), from_right)
        for q in range(6):
            drm[q, 0] = middle[q * HIGH_ROWS:(q + 1) * HIGH_ROWS, :]
            drm[q, 1] = edges[q * HIGH_ROWS:(q + 1) * HIGH_ROWS, :]

    def take_lanes():
        second = (lane & 4) != 0
        for g in range(len(y_planes) // GROUP):
            packed[g, core, :] = jnp.where(second, yr[0, g], yr[1, g])
            packed[g, top, :] = jnp.where(second[:8], corner[1, 1, g], corner[1, 0, g])
            packed[g, pl.ds(PAD + CX, 8), :] = jnp.where(second[:8], corner[0, 1, g], corner[0, 0, g])

    def unpack(planes):
        for plane in planes:
            name, f, z = plane
            ref = fields[name]
            k = x_planes.index(plane)
            m = y_planes.index(plane)
            back = CY - (2 * WIDE * (m % GROUP) + WIDE)
            if name == "zone":
                low = lookup(xr[1, k].astype(jnp.int32))
                high = lookup(xr[0, k].astype(jnp.int32))
                for t, target in enumerate(materials):
                    target[z, 0, PAD - WIDE:PAD, :] = low[t]
                    target[z, 0, PAD + CX:PAD + CX + WIDE, :] = high[t]
                    target[z, 1] = pltpu.roll(edge_materials[t], back, 1)
            else:
                ref[f, z, 0, PAD - WIDE:PAD, :] = xr[1, k]
                ref[f, z, 0, PAD + CX:PAD + CX + WIDE, :] = xr[0, k]
                ref[f, z, 1] = pltpu.roll(packed[m // GROUP], back, 1)

    def region(last):
        return (PAD, CX) if last else (PAD - WIDE, CX + 2 * WIDE)

    def diffs(ref, f, z, c, r, n):
        def at(k, d):
            return ref[f, k, c, pl.ds(r + d, n), :]

        def dx():
            return at(z, 1) - at(z, -1)

        def dz():
            if z == 0:
                return at(1, 0)
            if z == NZ - 1:
                return -at(NZ - 2, 0)
            return at(z + 1, 0) - at(z - 1, 0)

        def dy():
            here = wide_lane[:n]
            value, other = at(z, 0), ref[f, z, 1 - c, pl.ds(r, n), :]
            up = jnp.where(here == CY - 1, pltpu.roll(other, CY - 1, 1), pltpu.roll(value, CY - 1, 1))
            down = jnp.where(here == 0, pltpu.roll(other, 1, 1), pltpu.roll(value, 1, 1))
            return up - down

        return dx, dy, dz

    def velocity_planes(step, z0, z1):
        r, n = region(False)
        here = pl.ds(r, n)
        for z in range(z0, z1):
            for c in range(2):
                b = buoy[z, c, here, :]
                dxx, dxz, dxy, dyy, dyz, dzz = [diffs(S, f, z, c, r, n) for f in range(6)]
                force = [
                    dxx[0]() + dxy[1]() + dxz[2](),
                    dxy[0]() + dyy[1]() + dyz[2](),
                    dxz[0]() + dyz[1]() + dzz[2](),
                ]
                for k in range(3):
                    f = force[k]
                    if z == NZ - 1:
                        f = f + 20.0 * mu[z, c, here, :] * drm[step * 3 + k, c, here, :]
                    V[k, z, c, here, :] = V[k, z, c, here, :] + b * f

    def stress_planes(z0, z1, last):
        r, n = region(last)
        here = pl.ds(r, n)
        for z in range(z0, z1):
            for c in range(1 if last else 2):
                vx, vy, vz = [diffs(V, f, z, c, r, n) for f in range(3)]
                m1 = mu[z, c, here, :]
                dvx, dvy, dvz = vx[0](), vy[1](), vz[2]()
                common = lam[z, c, here, :] * (dvx + dvy + dvz)
                m2 = m1 + m1
                S[XX, z, c, here, :] = S[XX, z, c, here, :] + (common + m2 * dvx)
                S[YY, z, c, here, :] = S[YY, z, c, here, :] + (common + m2 * dvy)
                S[ZZ, z, c, here, :] = S[ZZ, z, c, here, :] + (common + m2 * dvz)
                S[XZ, z, c, here, :] = S[XZ, z, c, here, :] + m1 * (vx[2]() + vz[0]())
                S[XY, z, c, here, :] = S[XY, z, c, here, :] + m1 * (vx[1]() + vy[0]())
                S[YZ, z, c, here, :] = S[YZ, z, c, here, :] + m1 * (vy[2]() + vz[1]())

    for k in (0, 1, 4, 5, 6, 7, 8, 9):
        halo[k].wait_recv()
    take_lanes()
    edge_materials = lookup(packed[len(y_planes) // GROUP - 1].astype(jnp.int32))
    unpack(early)
    velocity_planes(0, 0, 5)
    stress_planes(0, 4, False)
    velocity_planes(1, 0, 3)
    stress_planes(0, 2, True)

    sums = jnp.concatenate(
        [jnp.sum(S[f, 1, 0, core, :].reshape(CX // BLOCK, BLOCK, CY), axis=1) for f in (XZ, YZ)], axis=0)
    fold_shape = (CY, n_blocks)
    fold = ((row_of(fold_shape) >> 3) == (lane_of(fold_shape) & 15)).astype(F32)
    per_block = jnp.dot(sums, fold, precision=HIGH, preferred_element_type=F32)
    mask_shape = (8, n_blocks)
    own_row = (row_of(mask_shape) & 3) == (lane_of(mask_shape) >> 4)
    per_block = jnp.where(own_row, per_block, 0.0) * (1.0 / (BLOCK * BLOCK))
    total = jnp.dot(per_block, counts[...], precision=HIGH, preferred_element_type=F32)
    per_owner = ROWS // owners
    for comp in range(2):
        row = jnp.sum(total[4 * comp:4 * comp + 4], axis=0, keepdims=True)
        for t in range(BUILDINGS // LANES):
            k = comp * (BUILDINGS // LANES) + t
            part[k // per_owner, k % per_owner] = row[:, t * LANES:(t + 1) * LANES]

    my_row = gy % owners

    def send_part(d, carry):
        to = (gy + d) % GY
        pltpu.make_async_remote_copy(
            src_ref=part.at[to % owners], dst_ref=r1.at[gy], send_sem=sum_sems.at[0],
            recv_sem=sum_sems.at[1], device_id=(gx, to), device_id_type=MESH).start()
        return carry

    lax.fori_loop(1, GY, send_part, 0)
    r1[gy] = part[my_row]
    lax.fori_loop(near, GX, send_higher, 0)
    peers_y = pl.ds(0, GY - 1)
    wait_r1 = whole(r1.at[peers_y], r1.at[peers_y], sum_sems.at[0], sum_sems.at[1])
    wait_r1.wait_recv()
    q1[...] = jnp.sum(r1[...], axis=0)

    is_hub = z_me == 0
    for x in range(x_size):
        @pl.when(gx != x * z_size)
        def _():
            pltpu.make_async_remote_copy(
                src_ref=q1, dst_ref=hub.at[gx], send_sem=sum_sems.at[2],
                recv_sem=sum_sems.at[3], device_id=(x * z_size, gy), device_id_type=MESH).start()

    halo[2].wait_recv()
    halo[3].wait_recv()
    unpack(late)
    share_block()

    peers_x = pl.ds(0, GX - 1)
    wait_hub = whole(hub.at[peers_x], hub.at[peers_x], sum_sems.at[2], sum_sems.at[3])

    def send_down(z, carry):
        pltpu.make_async_remote_copy(
            src_ref=q2, dst_ref=q2, send_sem=sum_sems.at[4],
            recv_sem=sum_sems.at[5], device_id=(base_x + z, gy), device_id_type=MESH).start()
        return carry

    down = whole(q2, q2, sum_sems.at[4], sum_sems.at[5])

    @pl.when(is_hub)
    def _():
        hub[gx] = q1[...]
        wait_hub.wait_recv()
        q2[...] = jnp.sum(hub[...], axis=0)
        lax.fori_loop(1, z_size, send_down, 0)

    @pl.when(z_me != 0)
    def _():
        down.wait_recv()

    base = gy - my_row

    def send_total(d, carry):
        to = base + (my_row + d) % owners
        pltpu.make_async_remote_copy(
            src_ref=q2, dst_ref=gathered.at[my_row], send_sem=sum_sems.at[6],
            recv_sem=sum_sems.at[7], device_id=(gx, to), device_id_type=MESH).start()
        return carry

    lax.fori_loop(1, owners, send_total, 0)
    gathered[my_row] = q2[...]

    spread_blocks()
    velocity_planes(0, 5, NZ)
    stress_planes(4, NZ, False)
    velocity_planes(1, 3, NZ)
    save_v = pltpu.make_async_copy(V.at[:, :, 0, core, :], vel_out, store_sem.at[0])
    save_v.start()
    stress_planes(2, NZ, True)
    save_s = pltpu.make_async_copy(S.at[:, :, 0, core, :], stress_out, store_sem.at[1])
    save_s.start()

    some = pl.ds(0, owners - 1)
    wait_g = whole(gathered.at[some], gathered.at[some], sum_sems.at[6], sum_sems.at[7])
    wait_g.wait_recv()
    for comp in range(2):
        for t in range(BUILDINGS // LANES):
            k = comp * (BUILDINGS // LANES) + t
            shear[comp:comp + 1, t * LANES:(t + 1) * LANES] = gathered[k // per_owner, k % per_owner]

    for copy in halo + share:
        copy.wait_send()
    all_regional.wait_send()
    wait_r1.wait_send()
    for x in range(x_size):
        @pl.when(gx != x * z_size)
        def _():
            down_like = whole(q1, q1, sum_sems.at[2], sum_sems.at[3])
            down_like.wait_send()

    @pl.when(is_hub)
    def _():
        low = whole(
            hub.at[pl.ds(0, z_size - 1)], hub.at[pl.ds(0, z_size - 1)], sum_sems.at[4], sum_sems.at[5])
        low.wait_send()

    wait_g.wait_send()
    save_v.wait()
    save_s.wait()


def body(velocity, stress, zones, zone_table, regional, owner, footprint_building, footprint_block):
    GX, GY = lax.axis_size("gx"), lax.axis_size("gy")
    owners = min(GY, ROWS)
    per_owner = ROWS // owners
    planes = 10 * NZ
    groups = planes // GROUP
    vmem = pl.BlockSpec(memory_space=pltpu.VMEM)
    hbm = pl.BlockSpec(memory_space=pltpu.HBM)
    dma = pltpu.SemaphoreType.DMA
    return pl.pallas_call(
        kernel,
        out_shape=(
            jax.ShapeDtypeStruct(velocity.shape, F32),
            jax.ShapeDtypeStruct(stress.shape, F32),
            jax.ShapeDtypeStruct((2, BUILDINGS), F32),
        ),
        in_specs=[hbm] * 8,
        out_specs=(hbm, hbm, vmem),
        scratch_shapes=[
            pltpu.VMEM((6, NZ, 2, HIGH_ROWS, CY), F32),
            pltpu.VMEM((3, NZ, 2, HIGH_ROWS, CY), F32),
            pltpu.VMEM((NZ, 2, HIGH_ROWS, CY), F32),
            pltpu.VMEM((NZ, 2, HIGH_ROWS, CY), F32),
            pltpu.VMEM((NZ, 2, HIGH_ROWS, CY), F32),
            pltpu.VMEM((6, 2, HIGH_ROWS, CY), F32),
            pltpu.VMEM((64, BUILDINGS), F32),
            pltpu.VMEM((2, planes, WIDE, CY), F32),
            pltpu.VMEM((2, planes, WIDE, CY), F32),
            pltpu.VMEM((groups, CX, CY), F32),
            pltpu.VMEM((2, groups, CX, CY), F32),
            pltpu.VMEM((2, 2, groups, 8, CY), F32),
            pltpu.VMEM((groups, HIGH_ROWS, CY), F32),
            pltpu.VMEM((3, 3, 6, 1, 2 * LANES), F32),
            pltpu.VMEM((GX, 6, 1, 2 * LANES), F32),
            pltpu.VMEM((GX, 6, 1, 2 * LANES), F32),
            pltpu.VMEM((owners, per_owner, 1, LANES), F32),
            pltpu.VMEM((GY, per_owner, 1, LANES), F32),
            pltpu.VMEM((per_owner, 1, LANES), F32),
            pltpu.VMEM((GX, per_owner, 1, LANES), F32),
            pltpu.VMEM((per_owner, 1, LANES), F32),
            pltpu.VMEM((owners, per_owner, 1, LANES), F32),
            pltpu.SMEM(owner.shape, owner.dtype),
            pltpu.SMEM(zone_table.shape, zone_table.dtype),
            pltpu.VMEM(zones.shape, zones.dtype),
            pltpu.VMEM(regional.shape, regional.dtype),
            pltpu.VMEM(footprint_building.shape, footprint_building.dtype),
            pltpu.VMEM(footprint_block.shape, footprint_block.dtype),
            dma((8,)),
            dma((2,)),
            dma((10,)),
            dma((10,)),
            dma((8,)),
            dma((8,)),
            dma((2,)),
            dma((8,)),
            pltpu.SemaphoreType.REGULAR((GX,)),
            pltpu.SemaphoreType.REGULAR((2, 3)),
        ],
        compiler_params=pltpu.CompilerParams(
            collective_id=0, has_side_effects=True, vmem_limit_bytes=60 * 1024 * 1024
        ),
    )(owner, zone_table, velocity, stress, zones, regional, footprint_building, footprint_block)


def solution(mesh):
    return jax.shard_map(
        body,
        mesh=mesh,
        in_specs=(
            P(None, None, "gx", "gy"),
            P(None, None, "gx", "gy"),
            P(None, "gx", "gy"),
            P(),
            P("gx", None, None, None, "gy"),
            P(),
            P("gx", "gy", None),
            P("gx", "gy", None),
        ),
        out_specs=(P(None, None, "gx", "gy"), P(None, None, "gx", "gy"), P()),
        check_vma=False,
    )
```

```python
import functools

import jax
import jax.numpy as jnp
from jax import lax
from jax.experimental import pallas as pl
from jax.experimental.pallas import tpu as pltpu
from jax.sharding import PartitionSpec as P

CX = 32
CY = 128
NZ = 8
STEPS = 2
COARSE = 4
BLOCK = 8
ZONES = 16
BUILDINGS = 1024
LANES = 128
PAD = 8
WIDE = 4
HIGH_ROWS = CX + 2 * PAD
GROUP = 16
ROWS = 2 * BUILDINGS // LANES
MESH = pl.DeviceIdType.MESH
HIGH = lax.Precision.HIGHEST
F32 = jnp.float32

XX, XZ, XY, YY, YZ, ZZ = range(6)


def lane_of(shape):
    return lax.broadcasted_iota(jnp.int32, shape, len(shape) - 1)


def row_of(shape):
    return lax.broadcasted_iota(jnp.int32, shape, len(shape) - 2)


def layers(gx_size):
    z_size = min(gx_size, 16)
    return z_size, gx_size // z_size


def kernel(
    owner_hbm, table_hbm, vel, stress_in, zones_hbm, regional_hbm, buildings_hbm, blocks_hbm,
    vel_out, stress_out, shear,
    S, V, lam, mu, buoy, drm, counts,
    xs, xr, ys, yr, corner, packed, block, reg_send, reg_recv, part, r1, q1, hub, q2, gathered,
    owner, table, zones, regional, buildings, blocks,
    load_sem, store_sem, halo_send, halo_recv, block_send, block_recv, reg_sems, sum_sems, entered, beside,
):
    GX, GY = lax.axis_size("gx"), lax.axis_size("gy")
    gx, gy = lax.axis_index("gx"), lax.axis_index("gy")
    z_size, x_size = layers(GX)
    owners = part.shape[0]
    z_me = gx % z_size
    base_x = gx - z_me

    def rank_of(g):
        return (g % z_size) * x_size + g // z_size

    def at_rank(q):
        return (q % x_size) * z_size + q // x_size

    me = rank_of(gx)

    core = pl.ds(PAD, CX)
    loads = [
        pltpu.make_async_copy(src, dst, load_sem.at[k]) for k, (src, dst) in enumerate([
            (stress_in, S.at[:, :, 0, core, :]), (vel, V.at[:, :, 0, core, :]), (regional_hbm, regional),
            (zones_hbm, zones), (table_hbm, table), (owner_hbm, owner), (buildings_hbm, buildings),
            (blocks_hbm, blocks),
        ])
    ]
    for load in loads:
        load.start()

    barrier = pltpu.get_barrier_semaphore()

    def greet_x(q, carry):
        pl.semaphore_signal(barrier, inc=1, device_id=(at_rank(q), gy), device_id_type=MESH)
        return carry

    def greet_y(d, carry):
        pl.semaphore_signal(barrier, inc=1, device_id=(gx, (gy + d) % GY), device_id_type=MESH)
        return carry

    after, before = (gx + 1) % GX, (gx + GX - 1) % GX
    right, left = (gy + 1) % GY, (gy + GY - 1) % GY
    sides = ((before, rank_of(before)), (after, rank_of(after)))

    for next_x, rank in sides:
        @pl.when(rank > me)
        def _():
            for y in (left, right):
                pl.semaphore_signal(barrier, inc=1, device_id=(next_x, y), device_id_type=MESH)

    lax.fori_loop(1, GY, greet_y, 0)
    lax.fori_loop(me + 1, GX, greet_x, 0)

    lower = [(rank < me).astype(jnp.int32) for _, rank in sides]
    pl.semaphore_wait(barrier, me + GY - 1 + 2 * (lower[0] + lower[1]))

    for side, (next_x, rank) in enumerate(sides):
        @pl.when(rank < me)
        def _():
            for k, y in enumerate((right, gy, left)):
                pl.semaphore_signal(
                    beside.at[1 - side, k], inc=1, device_id=(next_x, y), device_id_type=MESH)

    def answer(q, carry):
        pl.semaphore_signal(entered.at[me], inc=1, device_id=(at_rank(q), gy), device_id_type=MESH)
        return carry

    lax.fori_loop(0, me, answer, 0)

    lane = lane_of((CX, CY))
    wide_lane = lane_of((CX + 2 * WIDE, CY))

    fields = {"s": S, "v": V, "zone": zones}
    s_planes = [("s", f, z) for f in range(6) for z in range(NZ)]
    v_planes = [("v", f, z) for f in range(3) for z in range(NZ)]
    z_planes = [("zone", 0, z) for z in range(NZ)]
    y_planes = s_planes + v_planes + z_planes

    def needed_early(plane):
        name, f, z = plane
        return z < 5 or (name == "s" and f in (XZ, YZ, ZZ) and z < 6)

    early = [p for p in y_planes if needed_early(p)]
    late = [p for p in y_planes if not needed_early(p)]
    x_planes = early + late
    n_early = len(early)

    def rows_of(plane, r, n):
        name, f, z = plane
        if name == "zone":
            return zones[z, r:r + n, :].astype(F32)
        return fields[name][f, z, 0, PAD + r:PAD + r + n, :]

    for k in (0, 1, 3):
        loads[k].wait()
    for k, plane in enumerate(x_planes):
        xs[0, k] = rows_of(plane, 0, WIDE)
        xs[1, k] = rows_of(plane, CX - WIDE, WIDE)
    for g in range(len(y_planes) // GROUP):
        acc = jnp.zeros((CX, CY), F32)
        for k in range(GROUP):
            moved = pltpu.roll(rows_of(y_planes[g * GROUP + k], 0, CX), 2 * WIDE * k + WIDE, 1)
            acc = jnp.where((lane >> 3) == k, moved, acc)
        ys[g] = acc

    e_part, l_part = pl.ds(0, n_early), pl.ds(n_early, len(late))
    top, bottom = pl.ds(0, 8), pl.ds(CX - 8, 8)
    halo = [
        pltpu.make_async_remote_copy(
            src_ref=src, dst_ref=dst, send_sem=halo_send.at[k], recv_sem=halo_recv.at[k],
            device_id=to, device_id_type=MESH)
        for k, (src, dst, to) in enumerate([
            (xs.at[0, e_part], xr.at[0, e_part], (before, gy)),
            (xs.at[1, e_part], xr.at[1, e_part], (after, gy)),
            (xs.at[0, l_part], xr.at[0, l_part], (before, gy)),
            (xs.at[1, l_part], xr.at[1, l_part], (after, gy)),
            (ys, yr.at[0], (gx, left)),
            (ys, yr.at[1], (gx, right)),
            (ys.at[:, top, :], corner.at[0, 1], (before, left)),
            (ys.at[:, top, :], corner.at[0, 0], (before, right)),
            (ys.at[:, bottom, :], corner.at[1, 1], (after, left)),
            (ys.at[:, bottom, :], corner.at[1, 0], (after, right)),
        ])
    ]
    by_side = ((0, 6, 7, 2), (1, 8, 9, 3))

    for side, (next_x, rank) in enumerate(sides):
        @pl.when(rank < me)
        def _():
            for k in by_side[side]:
                halo[k].start()

    halo[4].start()
    halo[5].start()

    loads[2].wait()

    def pack_regional(i, carry):
        for s in range(STEPS):
            for c in range(3):
                reg_send[i, s * 3 + c, 0:1, :] = regional[0, s, c, pl.ds(i, 1), :]
        return carry

    lax.fori_loop(0, GX, pack_regional, 0)

    def send_regional(q):
        to = at_rank(q)
        pltpu.make_async_remote_copy(
            src_ref=reg_send.at[to], dst_ref=reg_recv.at[gx], send_sem=reg_sems.at[0],
            recv_sem=reg_sems.at[1], device_id=(to, gy), device_id_type=MESH).start()

    first_layer = 1 - jnp.minimum(z_me, 1)
    near = jnp.minimum(me + 1 + 3 * x_size + first_layer * GX, GX)

    def send_lower(q, carry):
        send_regional(q)
        return carry

    def send_higher(q, carry):
        pl.semaphore_wait(entered.at[q], 1)
        send_regional(q)
        return carry

    lax.fori_loop(0, me, send_lower, 0)
    reg_recv[gx] = reg_send[gx]

    for side, (next_x, rank) in enumerate(sides):
        @pl.when(rank > me)
        def _():
            for k in range(3):
                pl.semaphore_wait(beside.at[side, k], 1)
            for k in by_side[side]:
                halo[k].start()

    for k in (4, 5, 6, 7):
        loads[k].wait()

    def lookup(zone):
        bits = [(zone & (1 << b)) != 0 for b in range(4)]
        found = []
        for row in range(3):
            level = [table[row, t] * 0.1 for t in range(ZONES)]
            for b in range(4):
                level = [
                    jnp.where(bits[b], level[2 * t + 1], level[2 * t]) for t in range(len(level) // 2)
                ]
            found.append(level[0])
        return found

    materials = (lam, mu, buoy)
    for z in range(NZ):
        for target, value in zip(materials, lookup(zones[z])):
            target[z, 0, core, :] = value

    n_blocks = (CX // BLOCK) * (CY // BLOCK)
    entries = blocks.shape[-1]
    block_hot = (blocks[0] == row_of((n_blocks, entries))).astype(jnp.bfloat16)
    building_hot = (buildings[0] == row_of((BUILDINGS, entries))).astype(jnp.bfloat16)
    counts[...] = lax.dot_general(
        block_hot, building_hot, (((1,), (1,)), ((), ())), preferred_element_type=F32)

    lax.fori_loop(me + 1, near, send_higher, 0)

    def whole(src, dst, send_sem, recv_sem):
        return pltpu.make_async_remote_copy(
            src_ref=src, dst_ref=dst, send_sem=send_sem, recv_sem=recv_sem,
            device_id=((gx + 1) % GX, gy), device_id_type=MESH)

    all_regional = whole(
        reg_send.at[pl.ds(0, GX - 1)], reg_recv.at[pl.ds(0, GX - 1)], reg_sems.at[0], reg_sems.at[1])

    around = [(dx, dy) for dx in (-1, 0, 1) for dy in (-1, 0, 1) if (dx, dy) != (0, 0)]
    x_at, y_at = {-1: before, 0: gx, 1: after}, {-1: left, 0: gy, 1: right}
    share = [
        pltpu.make_async_remote_copy(
            src_ref=block.at[1, 1], dst_ref=block.at[1 - dx, 1 - dy], send_sem=block_send.at[k],
            recv_sem=block_recv.at[k], device_id=(x_at[dx], y_at[dy]), device_id_type=MESH)
        for k, (dx, dy) in enumerate(around)
    ]

    def share_block():
        all_regional.wait_recv()
        block[1, 1] = reg_recv[owner[gy]]
        for copy in share:
            copy.start()

    def spread_blocks():
        for copy in share:
            copy.wait_recv()
        wide = (HIGH_ROWS, 2 * LANES)
        row = row_of(wide)
        keep = (lane_of(wide) >> 5) == (((row - PAD) >> 2) & 7)

        def stack(y):
            parts = []
            for q in range(6):
                above, own, below = [jnp.broadcast_to(block[x, y, q], wide) for x in range(3)]
                value = jnp.where(row < PAD, above, jnp.where(row < PAD + CX, own, below))
                parts.append(jnp.where(keep, value, 0.0))
            return jnp.concatenate(parts, axis=0)

        shape = (2 * LANES, CY)
        cell, out = row_of(shape) & 31, lane_of(shape)
        own = (cell == (out >> 2)).astype(F32)
        from_left = ((cell == 31) & (out >= CY - WIDE)).astype(F32)
        from_right = ((cell == 0) & (out < WIDE)).astype(F32)
        dot = functools.partial(jnp.dot, precision=HIGH, preferred_element_type=F32)
        middle = dot(stack(1), own)
        edges = dot(stack(0), from_left) + dot(stack(2), from_right)
        for q in range(6):
            drm[q, 0] = middle[q * HIGH_ROWS:(q + 1) * HIGH_ROWS, :]
            drm[q, 1] = edges[q * HIGH_ROWS:(q + 1) * HIGH_ROWS, :]

    def take_lanes():
        second = (lane & 4) != 0
        for g in range(len(y_planes) // GROUP):
            packed[g, core, :] = jnp.where(second, yr[0, g], yr[1, g])
            packed[g, top, :] = jnp.where(second[:8], corner[1, 1, g], corner[1, 0, g])
            packed[g, pl.ds(PAD + CX, 8), :] = jnp.where(second[:8], corner[0, 1, g], corner[0, 0, g])

    def unpack(planes):
        for plane in planes:
            name, f, z = plane
            ref = fields[name]
            k = x_planes.index(plane)
            m = y_planes.index(plane)
            back = CY - (2 * WIDE * (m % GROUP) + WIDE)
            if name == "zone":
                low = lookup(xr[1, k].astype(jnp.int32))
                high = lookup(xr[0, k].astype(jnp.int32))
                for t, target in enumerate(materials):
                    target[z, 0, PAD - WIDE:PAD, :] = low[t]
                    target[z, 0, PAD + CX:PAD + CX + WIDE, :] = high[t]
                    target[z, 1] = pltpu.roll(edge_materials[t], back, 1)
            else:
                ref[f, z, 0, PAD - WIDE:PAD, :] = xr[1, k]
                ref[f, z, 0, PAD + CX:PAD + CX + WIDE, :] = xr[0, k]
                ref[f, z, 1] = pltpu.roll(packed[m // GROUP], back, 1)

    def region(last):
        return (PAD, CX) if last else (PAD - WIDE, CX + 2 * WIDE)

    def diffs(ref, f, z, c, r, n):
        def at(k, d):
            return ref[f, k, c, pl.ds(r + d, n), :]

        def dx():
            return at(z, 1) - at(z, -1)

        def dz():
            if z == 0:
                return at(1, 0)
            if z == NZ - 1:
                return -at(NZ - 2, 0)
            return at(z + 1, 0) - at(z - 1, 0)

        def dy():
            here = wide_lane[:n]
            value, other = at(z, 0), ref[f, z, 1 - c, pl.ds(r, n), :]
            up = pltpu.roll(jnp.where(here == 0, other, value), CY - 1, 1)
            down = pltpu.roll(jnp.where(here == CY - 1, other, value), 1, 1)
            return up - down

        return dx, dy, dz

    def velocity_planes(step, z0, z1):
        r, n = region(False)
        here = pl.ds(r, n)
        for z in range(z0, z1):
            for c in range(2):
                b = buoy[z, c, here, :]
                dxx, dxz, dxy, dyy, dyz, dzz = [diffs(S, f, z, c, r, n) for f in range(6)]
                force = [
                    dxx[0]() + dxy[1]() + dxz[2](),
                    dxy[0]() + dyy[1]() + dyz[2](),
                    dxz[0]() + dyz[1]() + dzz[2](),
                ]
                for k in range(3):
                    f = force[k]
                    if z == NZ - 1:
                        f = f + 20.0 * mu[z, c, here, :] * drm[step * 3 + k, c, here, :]
                    V[k, z, c, here, :] = V[k, z, c, here, :] + b * f

    def stress_planes(z0, z1, last):
        r, n = region(last)
        here = pl.ds(r, n)
        for z in range(z0, z1):
            for c in range(1 if last else 2):
                vx, vy, vz = [diffs(V, f, z, c, r, n) for f in range(3)]
                m1 = mu[z, c, here, :]
                dvx, dvy, dvz = vx[0](), vy[1](), vz[2]()
                common = lam[z, c, here, :] * (dvx + dvy + dvz)
                m2 = m1 + m1
                S[XX, z, c, here, :] = S[XX, z, c, here, :] + (common + m2 * dvx)
                S[YY, z, c, here, :] = S[YY, z, c, here, :] + (common + m2 * dvy)
                S[ZZ, z, c, here, :] = S[ZZ, z, c, here, :] + (common + m2 * dvz)
                S[XZ, z, c, here, :] = S[XZ, z, c, here, :] + m1 * (vx[2]() + vz[0]())
                S[XY, z, c, here, :] = S[XY, z, c, here, :] + m1 * (vx[1]() + vy[0]())
                S[YZ, z, c, here, :] = S[YZ, z, c, here, :] + m1 * (vy[2]() + vz[1]())

    for k in (0, 1, 4, 5, 6, 7, 8, 9):
        halo[k].wait_recv()
    take_lanes()
    edge_materials = lookup(packed[len(y_planes) // GROUP - 1].astype(jnp.int32))
    unpack(early)
    velocity_planes(0, 0, 5)
    stress_planes(0, 4, False)
    velocity_planes(1, 0, 3)
    stress_planes(0, 2, True)

    sums = jnp.concatenate(
        [jnp.sum(S[f, 1, 0, core, :].reshape(CX // BLOCK, BLOCK, CY), axis=1) for f in (XZ, YZ)], axis=0)
    fold_shape = (CY, n_blocks)
    fold = ((row_of(fold_shape) >> 3) == (lane_of(fold_shape) & 15)).astype(F32)
    per_block = jnp.dot(sums, fold, precision=HIGH, preferred_element_type=F32)
    mask_shape = (8, n_blocks)
    own_row = (row_of(mask_shape) & 3) == (lane_of(mask_shape) >> 4)
    per_block = jnp.where(own_row, per_block, 0.0) * (1.0 / (BLOCK * BLOCK))
    total = jnp.dot(per_block, counts[...], precision=HIGH, preferred_element_type=F32)
    per_owner = ROWS // owners
    for comp in range(2):
        row = jnp.sum(total[4 * comp:4 * comp + 4], axis=0, keepdims=True)
        for t in range(BUILDINGS // LANES):
            k = comp * (BUILDINGS // LANES) + t
            part[k // per_owner, k % per_owner] = row[:, t * LANES:(t + 1) * LANES]

    my_row = gy % owners

    def send_part(d, carry):
        to = (gy + d) % GY
        pltpu.make_async_remote_copy(
            src_ref=part.at[to % owners], dst_ref=r1.at[gy], send_sem=sum_sems.at[0],
            recv_sem=sum_sems.at[1], device_id=(gx, to), device_id_type=MESH).start()
        return carry

    lax.fori_loop(1, GY, send_part, 0)
    r1[gy] = part[my_row]
    lax.fori_loop(near, GX, send_higher, 0)
    peers_y = pl.ds(0, GY - 1)
    wait_r1 = whole(r1.at[peers_y], r1.at[peers_y], sum_sems.at[0], sum_sems.at[1])
    wait_r1.wait_recv()
    q1[...] = jnp.sum(r1[...], axis=0)

    is_hub = z_me == 0
    for x in range(x_size):
        @pl.when(gx != x * z_size)
        def _():
            pltpu.make_async_remote_copy(
                src_ref=q1, dst_ref=hub.at[gx], send_sem=sum_sems.at[2],
                recv_sem=sum_sems.at[3], device_id=(x * z_size, gy), device_id_type=MESH).start()

    share_block()

    peers_x = pl.ds(0, GX - 1)
    wait_hub = whole(hub.at[peers_x], hub.at[peers_x], sum_sems.at[2], sum_sems.at[3])

    def send_down(z, carry):
        pltpu.make_async_remote_copy(
            src_ref=q2, dst_ref=q2, send_sem=sum_sems.at[4],
            recv_sem=sum_sems.at[5], device_id=(base_x + z, gy), device_id_type=MESH).start()
        return carry

    down = whole(q2, q2, sum_sems.at[4], sum_sems.at[5])

    @pl.when(is_hub)
    def _():
        hub[gx] = q1[...]
        wait_hub.wait_recv()
        q2[...] = jnp.sum(hub[...], axis=0)
        lax.fori_loop(1, z_size, send_down, 0)

    @pl.when(z_me != 0)
    def _():
        down.wait_recv()

    base = gy - my_row

    def send_total(d, carry):
        to = base + (my_row + d) % owners
        pltpu.make_async_remote_copy(
            src_ref=q2, dst_ref=gathered.at[my_row], send_sem=sum_sems.at[6],
            recv_sem=sum_sems.at[7], device_id=(gx, to), device_id_type=MESH).start()
        return carry

    lax.fori_loop(1, owners, send_total, 0)
    gathered[my_row] = q2[...]

    halo[2].wait_recv()
    halo[3].wait_recv()
    unpack(late)
    spread_blocks()
    velocity_planes(0, 5, NZ)
    stress_planes(4, NZ, False)
    velocity_planes(1, 3, NZ)
    save_v = pltpu.make_async_copy(V.at[:, :, 0, core, :], vel_out, store_sem.at[0])
    save_v.start()
    stress_planes(2, NZ, True)
    save_s = pltpu.make_async_copy(S.at[:, :, 0, core, :], stress_out, store_sem.at[1])
    save_s.start()

    some = pl.ds(0, owners - 1)
    wait_g = whole(gathered.at[some], gathered.at[some], sum_sems.at[6], sum_sems.at[7])
    wait_g.wait_recv()
    for comp in range(2):
        for t in range(BUILDINGS // LANES):
            k = comp * (BUILDINGS // LANES) + t
            shear[comp:comp + 1, t * LANES:(t + 1) * LANES] = gathered[k // per_owner, k % per_owner]

    for copy in halo + share:
        copy.wait_send()
    all_regional.wait_send()
    wait_r1.wait_send()
    for x in range(x_size):
        @pl.when(gx != x * z_size)
        def _():
            down_like = whole(q1, q1, sum_sems.at[2], sum_sems.at[3])
            down_like.wait_send()

    @pl.when(is_hub)
    def _():
        low = whole(
            hub.at[pl.ds(0, z_size - 1)], hub.at[pl.ds(0, z_size - 1)], sum_sems.at[4], sum_sems.at[5])
        low.wait_send()

    wait_g.wait_send()
    save_v.wait()
    save_s.wait()


def move(v_in, s_in, b_in, v_out, s_out, b_out, v_mid, s_mid, b_mid, read_sem, write_sem):
    steps = []
    for src, mid, dst in ((b_in, b_mid, b_out), (v_in, v_mid, v_out), (s_in, s_mid, s_out)):
        parts = src.shape[0] if len(src.shape) > 2 else 1
        for k in range(parts):
            part = (src.at[k], mid.at[k], dst.at[k]) if parts > 1 else (src, mid, dst)
            n = len(steps)
            steps.append((
                pltpu.make_async_copy(part[0], part[1], read_sem.at[n]),
                pltpu.make_async_copy(part[1], part[2], write_sem.at[n]),
            ))
    for read, _ in steps:
        read.start()
    for read, write in steps:
        read.wait()
        write.start()
    for _, write in steps:
        write.wait()


def body(velocity, stress, zones, zone_table, regional, owner, footprint_building, footprint_block):
    GX, GY = lax.axis_size("gx"), lax.axis_size("gy")
    owners = min(GY, ROWS)
    per_owner = ROWS // owners
    planes = 10 * NZ
    groups = planes // GROUP
    vmem = pl.BlockSpec(memory_space=pltpu.VMEM)
    hbm = pl.BlockSpec(memory_space=pltpu.HBM)
    dma = pltpu.SemaphoreType.DMA
    results = pl.pallas_call(
        kernel,
        out_shape=(
            jax.ShapeDtypeStruct(velocity.shape, F32),
            jax.ShapeDtypeStruct(stress.shape, F32),
            jax.ShapeDtypeStruct((2, BUILDINGS), F32),
        ),
        in_specs=[hbm] * 8,
        out_specs=(hbm, hbm, vmem),
        scratch_shapes=[
            pltpu.VMEM((6, NZ, 2, HIGH_ROWS, CY), F32),
            pltpu.VMEM((3, NZ, 2, HIGH_ROWS, CY), F32),
            pltpu.VMEM((NZ, 2, HIGH_ROWS, CY), F32),
            pltpu.VMEM((NZ, 2, HIGH_ROWS, CY), F32),
            pltpu.VMEM((NZ, 2, HIGH_ROWS, CY), F32),
            pltpu.VMEM((6, 2, HIGH_ROWS, CY), F32),
            pltpu.VMEM((64, BUILDINGS), F32),
            pltpu.VMEM((2, planes, WIDE, CY), F32),
            pltpu.VMEM((2, planes, WIDE, CY), F32),
            pltpu.VMEM((groups, CX, CY), F32),
            pltpu.VMEM((2, groups, CX, CY), F32),
            pltpu.VMEM((2, 2, groups, 8, CY), F32),
            pltpu.VMEM((groups, HIGH_ROWS, CY), F32),
            pltpu.VMEM((3, 3, 6, 1, 2 * LANES), F32),
            pltpu.VMEM((GX, 6, 1, 2 * LANES), F32),
            pltpu.VMEM((GX, 6, 1, 2 * LANES), F32),
            pltpu.VMEM((owners, per_owner, 1, LANES), F32),
            pltpu.VMEM((GY, per_owner, 1, LANES), F32),
            pltpu.VMEM((per_owner, 1, LANES), F32),
            pltpu.VMEM((GX, per_owner, 1, LANES), F32),
            pltpu.VMEM((per_owner, 1, LANES), F32),
            pltpu.VMEM((owners, per_owner, 1, LANES), F32),
            pltpu.SMEM(owner.shape, owner.dtype),
            pltpu.SMEM(zone_table.shape, zone_table.dtype),
            pltpu.VMEM(zones.shape, zones.dtype),
            pltpu.VMEM(regional.shape, regional.dtype),
            pltpu.VMEM(footprint_building.shape, footprint_building.dtype),
            pltpu.VMEM(footprint_block.shape, footprint_block.dtype),
            dma((8,)),
            dma((2,)),
            dma((10,)),
            dma((10,)),
            dma((8,)),
            dma((8,)),
            dma((2,)),
            dma((8,)),
            pltpu.SemaphoreType.REGULAR((GX,)),
            pltpu.SemaphoreType.REGULAR((2, 3)),
        ],
        compiler_params=pltpu.CompilerParams(
            collective_id=0, has_side_effects=True, vmem_limit_bytes=60 * 1024 * 1024
        ),
    )(owner, zone_table, velocity, stress, zones, regional, footprint_building, footprint_block)
    return pl.pallas_call(
        move,
        out_shape=tuple(jax.ShapeDtypeStruct(r.shape, r.dtype) for r in results),
        in_specs=[hbm] * 3,
        out_specs=(hbm,) * 3,
        scratch_shapes=[pltpu.VMEM(r.shape, r.dtype) for r in results] + [dma((10,)), dma((10,))],
        compiler_params=pltpu.CompilerParams(vmem_limit_bytes=60 * 1024 * 1024),
    )(*results)


def solution(mesh):
    return jax.shard_map(
        body,
        mesh=mesh,
        in_specs=(
            P(None, None, "gx", "gy"),
            P(None, None, "gx", "gy"),
            P(None, "gx", "gy"),
            P(),
            P("gx", None, None, None, "gy"),
            P(),
            P("gx", "gy", None),
            P("gx", "gy", None),
        ),
        out_specs=(P(None, None, "gx", "gy"), P(None, None, "gx", "gy"), P()),
        check_vma=False,
    )
```
